256 devices in a mesh: row: 16 (over y_lo, x, core), col: 16 (over z, y_hi).
Axes of the slice: x: 4, y: 4 (y_hi: 2, y_lo: 2; y = y_hi * 2 + y_lo), z: 8, core: 2. Of those that a mesh axis runs over, the one named last changes fastest.
Arguments:
- row_frames: float32 [3, 8192, 256], P(None, ('row', 'col')), may hold values from -40 to 40, as said below
- col_frames: float32 [3, 8192, 256], P(None, ('col', 'row')), may hold values from -40 to 40, as said below
- vectors: float32 [64, 8192], P(None, ('col', 'row')), may hold values from -6 to 6
Outputs:
- embedding_product: float32 [64, 8192], P(None, ('row', 'col'))
The draws below stay inside these ranges and needn't reach their ends.
Inputs may be any that keep to these rules, and one draw needn't show every extreme that they name: `row_frames`: frames of one chain of 256 atoms, each rigidly rotated and moved and perturbed by its own amount. `col_frames`: frames of one chain of 256 atoms, each rigidly rotated and moved and perturbed by its own amount.
All inputs are finite; a program needn't handle non-finite values.
Results may differ from the reference program's by a relative error of at most 0.00017.
Values sent between devices are 32-bit elements; how exact they have to be, the bound alone decides.
A program may use at most 64 MiB of HBM per device.

```python
import math
import jax
import jax.numpy as jnp
from jax import lax

A = 256
NV = 64
NEWTON = 8
FR_DEV = 32
ROWS = 8192
COLS = 8192
N_ROW = 16
N_COL = 16


def make_frames(key, label, count):
    base = jax.random.truncated_normal(jax.random.fold_in(key, 11), -4.0, 4.0, (3, A)) * 3.0
    own_key = jax.random.fold_in(key, label)
    key_scale, key_noise, key_turn, key_shift = jax.random.split(own_key, 4)
    spread = jnp.exp(jax.random.uniform(key_scale, (count,), jnp.float32, math.log(0.3), math.log(1.2)))
    noise = jax.random.truncated_normal(key_noise, -4.0, 4.0, (3, count, A))
    shape_body = base[:, None, :] + spread[None, :, None] * noise
    quaternion = jax.random.normal(key_turn, (4, count))
    quaternion = quaternion / jnp.sqrt(jnp.sum(quaternion * quaternion, axis=0, keepdims=True) + 1e-06)
    quat_w, quat_x, quat_y, quat_z = (quaternion[0], quaternion[1], quaternion[2], quaternion[3])
    turn = [[1 - 2 * (quat_y * quat_y + quat_z * quat_z), 2 * (quat_x * quat_y - quat_z * quat_w), 2 * (quat_x * quat_z + quat_y * quat_w)], [2 * (quat_x * quat_y + quat_z * quat_w), 1 - 2 * (quat_x * quat_x + quat_z * quat_z), 2 * (quat_y * quat_z - quat_x * quat_w)], [2 * (quat_x * quat_z - quat_y * quat_w), 2 * (quat_y * quat_z + quat_x * quat_w), 1 - 2 * (quat_x * quat_x + quat_y * quat_y)]]
    shift = jax.random.uniform(key_shift, (3, count), jnp.float32, -10.0, 10.0)
    rotated = [turn[row_id][0][:, None] * shape_body[0] + turn[row_id][1][:, None] * shape_body[1] + turn[row_id][2][:, None] * shape_body[2] + shift[row_id][:, None] for row_id in range(3)]
    return jnp.stack(rotated, axis=0).astype(jnp.float32)


def draw_row_frames(key, part):
    return make_frames(key, 1, ROWS)


def draw_col_frames(key, part):
    return make_frames(key, 2, COLS)


def steps_of(key, shape, shards, low, top_value):
    factor_of, own = 1.0, jax.random.fold_in(key, 6)
    for axis_at, parts in shards:
        heights = jnp.exp(jax.random.uniform(jax.random.fold_in(own, axis_at), (parts,), jnp.float32, low / len(shards), top_value / len(shards)))
        factor_of = factor_of * jnp.repeat(heights, shape[axis_at] // parts).reshape([-1 if axis == axis_at else 1 for axis in range(len(shape))])
    return factor_of


def scatter_about(key, extent, scale, bound, cuts=(), kind=jnp.bfloat16):
    drawn = scale * jax.random.normal(key, extent, jnp.float32)
    if cuts:
        drawn = drawn * steps_of(key, extent, cuts, -0.22, 0.18)
    return jnp.clip(drawn, -bound, bound).astype(kind)


def setup_inputs(seed: int = 0) -> dict:
    keys = jax.random.split(jax.random.key(seed), 4)
    return {
        "row_frames": draw_row_frames(jax.random.fold_in(keys[3], 71), 0),
        "col_frames": draw_col_frames(jax.random.fold_in(keys[3], 71), 0),
        "vectors": scatter_about(keys[2], (NV, COLS), 1.0, 6.0, ((1, 256),), jnp.float32),
    }


band_width = 2.0


def centre(frames):
    return frames - jnp.mean(frames, axis=2, keepdims=True)


def kernel_tile(rows, cols):
    count_rows = rows.shape[1]
    count_cols = cols.shape[1]
    atoms = rows.shape[2]
    row_norms = jnp.sum(rows * rows, axis=(0, 2))
    col_norms = jnp.sum(cols * cols, axis=(0, 2))
    product = jnp.dot(cols.reshape(3 * count_cols, atoms), rows.reshape(3 * count_rows, atoms).T,
                      precision=lax.Precision.HIGHEST, preferred_element_type=jnp.float32)
    product = product.reshape(3, count_cols, 3, count_rows)
    moment = [[product[second, :, first, :] for second in range(3)] for first in range(3)]
    half_norm = 0.5 * (row_norms[None, :] + col_norms[:, None])
    coef_two = -2.0 * sum(moment[first][second] * moment[first][second] for first in range(3) for second in range(3))
    coef_one = 8.0 * (moment[0][0] * moment[1][2] * moment[2][1] + moment[1][1] * moment[2][0] * moment[0][2]
                      + moment[2][2] * moment[0][1] * moment[1][0]) - 8.0 * (
        moment[0][0] * moment[1][1] * moment[2][2] + moment[1][2] * moment[2][0] * moment[0][1]
        + moment[2][1] * moment[1][0] * moment[0][2])
    trace_one = moment[0][0] + moment[1][1] + moment[2][2]
    key_matrix = [
        [trace_one, moment[1][2] - moment[2][1], moment[2][0] - moment[0][2], moment[0][1] - moment[1][0]],
        [moment[1][2] - moment[2][1], moment[0][0] - moment[1][1] - moment[2][2], moment[0][1] + moment[1][0], moment[2][0] + moment[0][2]],
        [moment[2][0] - moment[0][2], moment[0][1] + moment[1][0], -moment[0][0] + moment[1][1] - moment[2][2], moment[1][2] + moment[2][1]],
        [moment[0][1] - moment[1][0], moment[2][0] + moment[0][2], moment[1][2] + moment[2][1], -moment[0][0] - moment[1][1] + moment[2][2]],
    ]
    upper = key_matrix
    minor_top = [upper[0][0] * upper[1][1] - upper[1][0] * upper[0][1],
                 upper[0][0] * upper[1][2] - upper[1][0] * upper[0][2],
                 upper[0][0] * upper[1][3] - upper[1][0] * upper[0][3],
                 upper[0][1] * upper[1][2] - upper[1][1] * upper[0][2],
                 upper[0][1] * upper[1][3] - upper[1][1] * upper[0][3],
                 upper[0][2] * upper[1][3] - upper[1][2] * upper[0][3]]
    minor_low = [upper[2][0] * upper[3][1] - upper[3][0] * upper[2][1],
                 upper[2][0] * upper[3][2] - upper[3][0] * upper[2][2],
                 upper[2][0] * upper[3][3] - upper[3][0] * upper[2][3],
                 upper[2][1] * upper[3][2] - upper[3][1] * upper[2][2],
                 upper[2][1] * upper[3][3] - upper[3][1] * upper[2][3],
                 upper[2][2] * upper[3][3] - upper[3][2] * upper[2][3]]
    coef_zero = (minor_top[0] * minor_low[5] - minor_top[1] * minor_low[4] + minor_top[2] * minor_low[3]
                 + minor_top[3] * minor_low[2] - minor_top[4] * minor_low[1] + minor_top[5] * minor_low[0])
    eigen = half_norm
    for newton_step in range(NEWTON):
        eigen_sq = eigen * eigen
        value = (eigen_sq + coef_two) * eigen_sq + coef_one * eigen + coef_zero
        slope = 4.0 * eigen_sq * eigen + 2.0 * coef_two * eigen + coef_one
        eigen = eigen - value / slope
    squared = jnp.maximum(2.0 * (half_norm - eigen) / atoms, 0.0)
    return jnp.exp(-squared / band_width)


def reference(row_frames, col_frames, vectors):
    centred_rows = centre(row_frames)
    centred_cols = centre(col_frames)
    block = FR_DEV * N_COL
    blocks = centred_rows.reshape(3, N_ROW, block, A).transpose(1, 0, 2, 3)

    def one_block(rows):
        tile = kernel_tile(rows, centred_cols)
        degree = jnp.sum(tile, axis=0)
        weighted = jnp.dot(vectors, tile, precision=lax.Precision.HIGHEST, preferred_element_type=jnp.float32)
        return weighted / degree[None, :]

    result = lax.map(one_block, blocks)
    return result.transpose(1, 0, 2).reshape(NV, N_ROW * block)
```

```python
import jax
import jax.numpy as jnp
from jax import lax
from jax.experimental import pallas as pl
from jax.experimental.pallas import tpu as pltpu
from jax.sharding import PartitionSpec as P

NEWTON = 8
ATOMS = 256
FRAMES = 32
SLICE = 32
MESH = pl.DeviceIdType.MESH

ROW_SLOTS = (
    (0, 0), (1, 0), (3, 0), (0, 1),
    (0, 3), (1, 1), (1, 3), (2, 0),
    (3, 1), (3, 3), (0, 2), (2, 1),
    (2, 3), (1, 2), (3, 2), (2, 2),
)
ROW_AT = {where: at for at, where in enumerate(ROW_SLOTS)}
COL_GROUPS = ((1, 7), (2, 6), (3, 5), (0, 4))


def row_source(slot):
    first, second = slot
    if second == 0:
        source = {1: (0, 0), 3: (0, 0), 2: (1, 0)}[first]
        return source, ((3, 0) if first in (1, 2) else (1, 0))
    if second == 1:
        return (first, 0), (0, 3)
    if second == 3:
        return (first, 0), (0, 1)
    if first < 2:
        return (first, 1), (0, 3)
    return (first, 3), (0, 1)


def split(value):
    high = value.astype(jnp.bfloat16)
    low = (value - high.astype(jnp.float32)).astype(jnp.bfloat16)
    return high, low


def kernel_values(moment, row_norm, col_norm):
    s00, s01, s02, s10, s11, s12, s20, s21, s22 = moment
    cof = (
        s11 * s22 - s12 * s21, s12 * s20 - s10 * s22, s10 * s21 - s11 * s20,
        s02 * s21 - s01 * s22, s00 * s22 - s02 * s20, s01 * s20 - s00 * s21,
        s01 * s12 - s02 * s11, s02 * s10 - s00 * s12, s00 * s11 - s01 * s10,
    )
    total = s00 * s00
    for entry in moment[1:]:
        total = total + entry * entry
    minors = cof[0] * cof[0]
    for entry in cof[1:]:
        minors = minors + entry * entry
    coef_two = -2.0 * total
    coef_one = -8.0 * (s00 * cof[0] + s01 * cof[1] + s02 * cof[2])
    coef_zero = total * total - 4.0 * minors
    half_norm = 0.5 * (row_norm + col_norm)
    eigen = half_norm
    for _ in range(NEWTON):
        square = eigen * eigen
        inner = square + coef_two
        cubic = inner * eigen + coef_one
        value = cubic * eigen + coef_zero
        slope = cubic + eigen * (inner + (square + square))
        eigen = eigen - value / slope
    return jnp.exp(jnp.minimum((eigen - half_norm) * (1.0 / ATOMS), 0.0))


def body(
    rows_ref, cols_ref, vec_ref, out_ref,
    rbuf, cbuf, rsplit, csplit, vsplit, rnorm, cnorm, moments, acc, parts, landed, square_buf,
    rsend, rrecv, csend, crecv, psend, precv, ssend, srecv,
):
    row, col = lax.axis_index("row"), lax.axis_index("col")
    core = lax.rem(row, 2)
    at_x = lax.rem(lax.div(row, 2), 4)
    at_y = lax.rem(col, 2) * 2 + lax.div(row, 8)
    at_z = lax.div(col, 2)

    def device(first, second, along=0, other=False):
        to_x = lax.rem(at_x + (1 - core) * first + core * (4 - second), 4)
        to_y = lax.rem(at_y + (1 - core) * second + core * (4 - first), 4)
        to_z = lax.rem(at_z + (1 - core) * along + core * (8 - along), 8)
        to_core = 1 - core if other else core
        to_row = (lax.rem(to_y, 2) * 4 + to_x) * 2 + to_core
        return (to_row, to_z * 2 + lax.div(to_y, 2))

    neighbours = (
        device(1, 0), device(3, 0), device(0, 1), device(0, 3),
        device(0, 0, 1), device(0, 0, 7), device(0, 0, 0, True),
    )
    barrier = pltpu.get_barrier_semaphore()
    for neighbour in neighbours:
        pl.semaphore_signal(barrier, inc=1, device_id=neighbour, device_id_type=MESH)

    def row_copy(slot):
        source, toward = row_source(slot)
        at = ROW_AT[slot]
        return pltpu.make_async_remote_copy(
            src_ref=rbuf.at[ROW_AT[source]], dst_ref=rbuf.at[at],
            send_sem=rsend.at[at], recv_sem=rrecv.at[at],
            device_id=device(*toward), device_id_type=MESH,
        )

    def col_copy(slot):
        source, toward = (slot - 1, 7) if slot <= 4 else ((slot + 1) % 8, 1)
        return pltpu.make_async_remote_copy(
            src_ref=cbuf.at[0, source], dst_ref=cbuf.at[0, slot],
            send_sem=csend.at[slot], recv_sem=crecv.at[slot],
            device_id=device(0, 0, toward), device_id_type=MESH,
        )

    def pair_copy(slot):
        return pltpu.make_async_remote_copy(
            src_ref=cbuf.at[0, slot], dst_ref=cbuf.at[1, slot],
            send_sem=psend.at[slot], recv_sem=precv.at[slot],
            device_id=device(0, 0, 0, True), device_id_type=MESH,
        )

    def share_copy(at):
        return pltpu.make_async_remote_copy(
            src_ref=parts.at[at], dst_ref=landed.at[at],
            send_sem=ssend.at[at], recv_sem=srecv.at[at],
            device_id=device(*ROW_SLOTS[at]), device_id_type=MESH,
        )

    for comp in range(3):
        frames = rows_ref[comp]
        rbuf[0, comp * FRAMES:(comp + 1) * FRAMES, :] = frames - jnp.mean(frames, axis=1, keepdims=True)
        frames = cols_ref[comp]
        cbuf[0, 0, comp * FRAMES:(comp + 1) * FRAMES, :] = frames - jnp.mean(frames, axis=1, keepdims=True)
    square_buf[...] = jnp.zeros_like(square_buf)
    square_buf[0:64, 0:FRAMES] = vec_ref[...]
    square_buf[64:72, :] = jnp.ones((8, 128), jnp.float32)
    turned = square_buf[...].T
    cbuf[0, 0, 96:112, 0:128] = turned[0:16, :]
    cbuf[0, 0, 96:112, 128:256] = turned[16:32, :]
    acc[...] = jnp.zeros_like(acc)

    pl.semaphore_wait(barrier, len(neighbours))

    for slot in ((1, 0), (3, 0), (0, 1), (0, 3)):
        row_copy(slot).start()
    col_copy(1).start()
    col_copy(7).start()
    pair_copy(0).start()

    def prepare_rows(chunk):
        for place in range(4):
            norm = jnp.zeros((FRAMES, 1), jnp.float32)
            for comp in range(3):
                value = rbuf[4 * chunk + place, comp * FRAMES:(comp + 1) * FRAMES, :]
                norm = norm + jnp.sum(value * value, axis=1, keepdims=True)
                high, low = split(value)
                at = pl.ds(comp * 128 + place * FRAMES, FRAMES)
                rsplit[chunk, at, 0:256] = high
                rsplit[chunk, at, 256:512] = high
                rsplit[chunk, at, 512:768] = low
            rnorm[chunk, place * FRAMES:(place + 1) * FRAMES, :] = jnp.broadcast_to(norm, (FRAMES, 128))

    def prepare_cols(group):
        for place in range(4):
            kind, slot = place // 2, COL_GROUPS[group][place % 2]
            norm = jnp.zeros((FRAMES, 1), jnp.float32)
            for comp in range(3):
                value = cbuf[kind, slot, comp * FRAMES:(comp + 1) * FRAMES, :]
                norm = norm + jnp.sum(value * value, axis=1, keepdims=True)
                high, low = split(value)
                at = pl.ds(comp * 128 + place * FRAMES, FRAMES)
                csplit[group, at, 0:256] = high
                csplit[group, at, 256:512] = low
                csplit[group, at, 512:768] = high
            square_buf[place * FRAMES:(place + 1) * FRAMES, :] = jnp.broadcast_to(norm, (FRAMES, 128))
            for half in range(2):
                value = cbuf[kind, slot, 96:112, half * 128:(half + 1) * 128]
                high, low = split(value)
                start = place * FRAMES + half * 16
                vsplit[group, start:start + 16, :] = high
                vsplit[group, 128 + start:128 + start + 16, :] = high
                vsplit[group, 256 + start:256 + start + 16, :] = low
        cnorm[group] = square_buf[...].T[0:8, :]

    def unit(chunk, group):
        moments[...] = lax.dot_general(
            rsplit[chunk], csplit[group], (((1,), (1,)), ((), ())),
            preferred_element_type=jnp.float32,
        )
        col_norm = cnorm[group][0:1, :]
        for start in range(0, 128, SLICE):
            moment = [
                moments[first * 128 + start:first * 128 + start + SLICE, second * 128:(second + 1) * 128]
                for first in range(3) for second in range(3)
            ]
            values = kernel_values(moment, rnorm[chunk, start:start + SLICE, :], col_norm)
            high, low = split(values)
            joined = jnp.concatenate([high, low, high], axis=1)
            at = pl.ds(start, SLICE)
            acc[chunk, at, :] = acc[chunk, at, :] + jnp.dot(
                joined, vsplit[group], preferred_element_type=jnp.float32
            )

    def units(count, which):
        def step(index, carry):
            unit(*which(index))
            return carry
        lax.fori_loop(0, count, step, 0)

    def share(chunk):
        for place in range(4):
            at = 4 * chunk + place
            value = acc[chunk, place * FRAMES:(place + 1) * FRAMES, :]
            if at == 0:
                landed[0] = value
            else:
                parts[at] = value
                share_copy(at).start()

    col_copy(1).wait_recv()
    col_copy(2).start()
    pair_copy(1).start()
    col_copy(7).wait_recv()
    col_copy(6).start()
    pair_copy(7).start()
    row_copy((1, 0)).wait_recv()
    for slot in ((2, 0), (1, 1), (1, 3)):
        row_copy(slot).start()
    row_copy((3, 0)).wait_recv()
    for slot in ((3, 1), (3, 3)):
        row_copy(slot).start()
    row_copy((0, 1)).wait_recv()
    row_copy((0, 2)).start()
    prepare_rows(0)
    pair_copy(1).wait_recv()
    pair_copy(7).wait_recv()
    prepare_cols(0)
    units(1, lambda index: (0, 0))

    col_copy(2).wait_recv()
    col_copy(3).start()
    pair_copy(2).start()
    col_copy(6).wait_recv()
    col_copy(5).start()
    pair_copy(6).start()
    row_copy((2, 0)).wait_recv()
    for slot in ((2, 1), (2, 3)):
        row_copy(slot).start()
    row_copy((1, 1)).wait_recv()
    row_copy((1, 2)).start()
    row_copy((3, 3)).wait_recv()
    row_copy((3, 2)).start()
    row_copy((0, 3)).wait_recv()
    row_copy((1, 3)).wait_recv()
    prepare_rows(1)
    pair_copy(2).wait_recv()
    pair_copy(6).wait_recv()
    prepare_cols(1)
    units(3, lambda index: (jnp.minimum(index, 1), jnp.minimum(2 - index, 1)))

    col_copy(3).wait_recv()
    col_copy(4).start()
    pair_copy(3).start()
    col_copy(5).wait_recv()
    pair_copy(5).start()
    row_copy((2, 3)).wait_recv()
    row_copy((2, 2)).start()
    for slot in ((3, 1), (0, 2), (2, 1)):
        row_copy(slot).wait_recv()
    prepare_rows(2)
    pair_copy(3).wait_recv()
    pair_copy(5).wait_recv()
    prepare_cols(2)
    units(5, lambda index: (jnp.minimum(index, 2), jnp.minimum(4 - index, 2)))

    col_copy(4).wait_recv()
    pair_copy(4).start()
    for slot in ((1, 2), (3, 2), (2, 2)):
        row_copy(slot).wait_recv()
    prepare_rows(3)
    pair_copy(0).wait_recv()
    pair_copy(4).wait_recv()
    prepare_cols(3)
    units(4, lambda index: (3, index))
    share(3)
    for chunk in (2, 1, 0):
        units(1, lambda index, chunk=chunk: (chunk, 3))
        share(chunk)

    for slot in ROW_SLOTS[1:]:
        row_copy(slot).wait_send()
    for slot in range(1, 8):
        col_copy(slot).wait_send()
    for slot in range(8):
        pair_copy(slot).wait_send()
    total = landed[0]
    for at in range(15, 0, -1):
        share_copy(at).wait_recv()
        total = total + landed[at]
    square_buf[0:FRAMES, :] = total / total[:, 64:65]
    out_ref[...] = square_buf[...].T[0:64, 0:FRAMES]
    for at in range(1, 16):
        share_copy(at).wait_send()


def per_device(row_frames, col_frames, vectors):
    vmem = pl.BlockSpec(memory_space=pltpu.VMEM)
    dma = pltpu.SemaphoreType.DMA
    return pl.pallas_call(
        body,
        name="qcp_product",
        out_shape=jax.ShapeDtypeStruct(vectors.shape, jnp.float32),
        in_specs=[vmem] * 3,
        out_specs=vmem,
        scratch_shapes=[
            pltpu.VMEM((16, 96, ATOMS), jnp.float32),
            pltpu.VMEM((2, 8, 112, ATOMS), jnp.float32),
            pltpu.VMEM((4, 384, 768), jnp.bfloat16),
            pltpu.VMEM((4, 384, 768), jnp.bfloat16),
            pltpu.VMEM((4, 384, 128), jnp.bfloat16),
            pltpu.VMEM((4, 128, 128), jnp.float32),
            pltpu.VMEM((4, 8, 128), jnp.float32),
            pltpu.VMEM((384, 384), jnp.float32),
            pltpu.VMEM((4, 128, 128), jnp.float32),
            pltpu.VMEM((16, FRAMES, 128), jnp.float32),
            pltpu.VMEM((16, FRAMES, 128), jnp.float32),
            pltpu.VMEM((128, 128), jnp.float32),
            dma((16,)), dma((16,)), dma((8,)), dma((8,)),
            dma((8,)), dma((8,)), dma((16,)), dma((16,)),
        ],
        compiler_params=pltpu.CompilerParams(
            collective_id=0, has_side_effects=True, vmem_limit_bytes=40 << 20,
        ),
    )(row_frames, col_frames, vectors)


def solution(mesh):
    return jax.shard_map(
        per_device,
        mesh=mesh,
        in_specs=(
            P(None, ("row", "col"), None),
            P(None, ("col", "row"), None),
            P(None, ("col", "row")),
        ),
        out_specs=P(None, ("row", "col")),
        check_vma=False,
    )
```

```python
import jax
import jax.numpy as jnp
from jax import lax
from jax.experimental import pallas as pl
from jax.experimental.pallas import tpu as pltpu
from jax.sharding import PartitionSpec as P

NEWTON = 8
ATOMS = 256
FRAMES = 32
SLICE = 32
MESH = pl.DeviceIdType.MESH

ROW_SLOTS = (
    (0, 0), (1, 0), (3, 0), (0, 1),
    (0, 3), (1, 1), (1, 3), (2, 0),
    (3, 1), (3, 3), (0, 2), (2, 1),
    (2, 3), (1, 2), (3, 2), (2, 2),
)
ROW_AT = {where: at for at, where in enumerate(ROW_SLOTS)}
COL_GROUPS = ((1, 7), (2, 6), (3, 5), (0, 4))


def row_source(slot):
    first, second = slot
    if second == 0:
        source = {1: (0, 0), 3: (0, 0), 2: (1, 0)}[first]
        return source, ((3, 0) if first in (1, 2) else (1, 0))
    if second == 1:
        return (first, 0), (0, 3)
    if second == 3:
        return (first, 0), (0, 1)
    if first < 2:
        return (first, 1), (0, 3)
    return (first, 3), (0, 1)


def split(value):
    high = value.astype(jnp.bfloat16)
    low = (value - high.astype(jnp.float32)).astype(jnp.bfloat16)
    return high, low


def kernel_values(moment, row_norm, col_norm):
    s00, s01, s02, s10, s11, s12, s20, s21, s22 = moment
    g00 = s00 * s00 + s10 * s10 + s20 * s20
    g11 = s01 * s01 + s11 * s11 + s21 * s21
    g22 = s02 * s02 + s12 * s12 + s22 * s22
    g01 = s00 * s01 + s10 * s11 + s20 * s21
    g02 = s00 * s02 + s10 * s12 + s20 * s22
    g12 = s01 * s02 + s11 * s12 + s21 * s22
    pair = g11 + g22
    trace = g00 + pair
    minors = g00 * pair + g11 * g22 - (g01 * g01 + g02 * g02 + g12 * g12)
    det = s00 * (s11 * s22 - s12 * s21) + s01 * (s12 * s20 - s10 * s22) + s02 * (s10 * s21 - s11 * s20)
    half_trace = 0.5 * trace
    free = half_trace * half_trace - minors
    det_two = det + det
    full_norm = row_norm + col_norm
    eigen = full_norm
    for _ in range(NEWTON):
        square = eigen * eigen
        upper = (0.75 * square - half_trace) * square - free
        lower = (square - trace) * eigen - det_two
        eigen = upper / lower
    return jnp.exp(jnp.minimum((eigen - full_norm) * (0.5 / ATOMS), 0.0))


ROW_PIECES = ((0, 32), (32, 32), (64, 32))
COL_PIECES = ((0, 32), (32, 32), (64, 48))
UNITS = (
    ((0, 0),),
    ((0, 1), (1, 1), (1, 0)),
    ((0, 2), (1, 2), (2, 2), (2, 1), (2, 0)),
    ((3, 0), (3, 1), (3, 2), (3, 3), (2, 3), (1, 3), (0, 3)),
)


def body(
    rows_hbm, cols_hbm, vec_hbm, out_ref,
    rows_ref, cols_ref, vec_ref,
    rbuf, cbuf, rsplit, csplit, vsplit, rnorm, cnorm, moments_a, moments_b, ksplit_a, ksplit_b,
    acc, parts, landed, square_buf,
    isem, rsend, rrecv, csend, crecv, psend, precv, ssend, srecv,
):
    row, col = lax.axis_index("row"), lax.axis_index("col")
    core = lax.rem(row, 2)
    at_x = lax.rem(lax.div(row, 2), 4)
    at_y = lax.rem(col, 2) * 2 + lax.div(row, 8)
    at_z = lax.div(col, 2)

    def device(first, second, along=0, other=False):
        to_x = lax.rem(at_x + (1 - core) * first + core * (4 - second), 4)
        to_y = lax.rem(at_y + (1 - core) * second + core * (4 - first), 4)
        to_z = lax.rem(at_z + (1 - core) * along + core * (8 - along), 8)
        to_core = 1 - core if other else core
        to_row = (lax.rem(to_y, 2) * 4 + to_x) * 2 + to_core
        return (to_row, to_z * 2 + lax.div(to_y, 2))

    neighbours = (
        device(1, 0), device(3, 0), device(0, 1), device(0, 3),
        device(0, 0, 1), device(0, 0, 7), device(0, 0, 0, True),
    )
    barrier = pltpu.get_barrier_semaphore()
    for neighbour in neighbours:
        pl.semaphore_signal(barrier, inc=1, device_id=neighbour, device_id_type=MESH)
    loads = (
        pltpu.make_async_copy(rows_hbm, rows_ref, isem.at[0]),
        pltpu.make_async_copy(cols_hbm, cols_ref, isem.at[1]),
        pltpu.make_async_copy(vec_hbm, vec_ref, isem.at[2]),
    )
    for load in loads:
        load.start()

    def row_copy(slot, piece):
        source, toward = row_source(slot)
        at, span = ROW_AT[slot], pl.ds(*ROW_PIECES[piece])
        return pltpu.make_async_remote_copy(
            src_ref=rbuf.at[ROW_AT[source], span], dst_ref=rbuf.at[at, span],
            send_sem=rsend.at[at, piece], recv_sem=rrecv.at[at, piece],
            device_id=device(*toward), device_id_type=MESH,
        )

    def col_copy(slot, piece):
        source, toward = (slot - 1, 7) if slot <= 4 else ((slot + 1) % 8, 1)
        span = pl.ds(*COL_PIECES[piece])
        return pltpu.make_async_remote_copy(
            src_ref=cbuf.at[0, source, span], dst_ref=cbuf.at[0, slot, span],
            send_sem=csend.at[slot, piece], recv_sem=crecv.at[slot, piece],
            device_id=device(0, 0, toward), device_id_type=MESH,
        )

    def pair_copy(slot, piece):
        span = pl.ds(*COL_PIECES[piece])
        return pltpu.make_async_remote_copy(
            src_ref=cbuf.at[0, slot, span], dst_ref=cbuf.at[1, slot, span],
            send_sem=psend.at[slot, piece], recv_sem=precv.at[slot, piece],
            device_id=device(0, 0, 0, True), device_id_type=MESH,
        )

    def share_copy(at):
        return pltpu.make_async_remote_copy(
            src_ref=parts.at[at], dst_ref=landed.at[at],
            send_sem=ssend.at[at], recv_sem=srecv.at[at],
            device_id=device(*ROW_SLOTS[at]), device_id_type=MESH,
        )

    square_buf[...] = jnp.zeros_like(square_buf)
    square_buf[64:72, :] = jnp.ones((8, 128), jnp.float32)
    loads[0].wait()
    for comp in range(3):
        frames = rows_ref[comp]
        centred = frames - jnp.mean(frames, axis=1, keepdims=True)
        rbuf[0, comp * FRAMES:(comp + 1) * FRAMES, :] = centred + centred
    loads[1].wait()
    for comp in range(3):
        frames = cols_ref[comp]
        cbuf[0, 0, comp * FRAMES:(comp + 1) * FRAMES, :] = frames - jnp.mean(frames, axis=1, keepdims=True)
    loads[2].wait()
    square_buf[0:64, 0:FRAMES] = vec_ref[...]
    turned = square_buf[...].T
    cbuf[0, 0, 96:112, 0:128] = turned[0:16, :]
    cbuf[0, 0, 96:112, 128:256] = turned[16:32, :]

    pl.semaphore_wait(barrier, len(neighbours))

    for piece in range(3):
        for slot in ((1, 0), (3, 0), (0, 1), (0, 3)):
            row_copy(slot, piece).start()
        col_copy(1, piece).start()
        col_copy(7, piece).start()
        pair_copy(0, piece).start()

    def pass_on(piece, cols, rows):
        for slot, onward in cols:
            col_copy(slot, piece).wait_recv()
            if onward is not None:
                col_copy(onward, piece).start()
            pair_copy(slot, piece).start()
        for slot, onward in rows:
            row_copy(slot, piece).wait_recv()
            for later in onward:
                row_copy(later, piece).start()

    def first_round(piece):
        pass_on(piece, ((1, 2), (7, 6)), (
            ((1, 0), ((2, 0), (1, 1), (1, 3))), ((3, 0), ((3, 1), (3, 3))), ((0, 1), ((0, 2),)),
        ))

    def second_round(piece):
        pass_on(piece, ((2, 3), (6, 5)), (
            ((2, 0), ((2, 1), (2, 3))), ((1, 1), ((1, 2),)), ((3, 3), ((3, 2),)),
        ))

    def third_round(piece):
        pass_on(piece, ((3, 4), (5, None)), (((2, 3), ((2, 2),)),))

    def settle(rows, cols):
        for piece in range(3):
            for slot in rows:
                row_copy(slot, piece).wait_recv()
            for slot in cols:
                pair_copy(slot, piece).wait_recv()

    def prepare_rows(chunk):
        for place in range(4):
            norm = jnp.zeros((FRAMES, 1), jnp.float32)
            for comp in range(3):
                value = rbuf[4 * chunk + place, comp * FRAMES:(comp + 1) * FRAMES, :]
                norm = norm + jnp.sum(value * value, axis=1, keepdims=True)
                high, low = split(value)
                at = pl.ds(comp * 128 + place * FRAMES, FRAMES)
                rsplit[chunk, at, 0:256] = high
                rsplit[chunk, at, 256:512] = high
                rsplit[chunk, at, 512:768] = low
            rnorm[chunk, place * FRAMES:(place + 1) * FRAMES, :] = jnp.broadcast_to(0.25 * norm, (FRAMES, 128))

    def prepare_cols(group):
        for place in range(4):
            kind, slot = place // 2, COL_GROUPS[group][place % 2]
            norm = jnp.zeros((FRAMES, 1), jnp.float32)
            for comp in range(3):
                value = cbuf[kind, slot, comp * FRAMES:(comp + 1) * FRAMES, :]
                norm = norm + jnp.sum(value * value, axis=1, keepdims=True)
                high, low = split(value)
                at = pl.ds(comp * 128 + place * FRAMES, FRAMES)
                csplit[group, at, 0:256] = high
                csplit[group, at, 256:512] = low
                csplit[group, at, 512:768] = high
            square_buf[place * FRAMES:(place + 1) * FRAMES, :] = jnp.broadcast_to(norm, (FRAMES, 128))
            for half in range(2):
                value = cbuf[kind, slot, 96:112, half * 128:(half + 1) * 128]
                high, low = split(value)
                start = place * FRAMES + half * 16
                vsplit[group, start:start + 16, :] = high
                vsplit[group, 128 + start:128 + start + 16, :] = high
                vsplit[group, 256 + start:256 + start + 16, :] = low
        cnorm[group] = square_buf[...].T[0:8, :]

    def share(chunk):
        for place in range(4):
            at = 4 * chunk + place
            value = acc[chunk, place * FRAMES:(place + 1) * FRAMES, :]
            if at == 0:
                landed[0] = value
            else:
                parts[at] = value
                share_copy(at).start()

    moments, ksplit = (moments_a, moments_b), (ksplit_a, ksplit_b)
    started, flight = set(), {"moments": None, "values": None, "count": 0}

    def advance(unit):
        count = flight["count"]
        if unit is not None:
            moments[count % 2][...] = lax.dot_general(
                rsplit[unit[0]], csplit[unit[1]], (((1,), (1,)), ((), ())),
                preferred_element_type=jnp.float32,
            )
        valued = flight["values"]
        if valued is not None:
            chunk, group = valued
            added = jnp.dot(ksplit[count % 2][...], vsplit[group], preferred_element_type=jnp.float32)
            acc[chunk] = acc[chunk] + added if chunk in started else added
            started.add(chunk)
        ready = flight["moments"]
        if ready is not None:
            chunk, group = ready
            held, into = moments[(count + 1) % 2], ksplit[(count + 1) % 2]
            col_norm = cnorm[group][0:1, :]
            for start in range(0, 128, SLICE):
                moment = [
                    held[first * 128 + start:first * 128 + start + SLICE, second * 128:(second + 1) * 128]
                    for first in range(3) for second in range(3)
                ]
                values = kernel_values(moment, rnorm[chunk, start:start + SLICE, :], col_norm)
                high, low = split(values)
                into[start:start + SLICE, 0:128] = high
                into[start:start + SLICE, 128:256] = low
                into[start:start + SLICE, 256:384] = high
        if valued is not None and valued[1] == 3:
            share(valued[0])
        flight["moments"], flight["values"], flight["count"] = unit, ready, count + 1

    for piece in range(3):
        first_round(piece)
    settle((), (1, 7))
    prepare_rows(0)
    prepare_cols(0)
    second_round(0)
    advance(UNITS[0][0])
    second_round(1)
    second_round(2)
    settle(((0, 3), (1, 3)), (2, 6))
    prepare_rows(1)
    prepare_cols(1)
    for piece in range(3):
        advance(UNITS[1][piece])
        third_round(piece)
    settle(((3, 1), (0, 2), (2, 1)), (3, 5))
    prepare_rows(2)
    prepare_cols(2)
    for at, unit in enumerate(UNITS[2]):
        advance(unit)
        if 1 <= at <= 3:
            col_copy(4, at - 1).wait_recv()
            pair_copy(4, at - 1).start()
    settle(((1, 2), (3, 2), (2, 2)), (0, 4))
    prepare_rows(3)
    prepare_cols(3)
    for unit in UNITS[3]:
        advance(unit)
    advance(None)
    advance(None)

    for piece in range(3):
        for slot in ROW_SLOTS[1:]:
            row_copy(slot, piece).wait_send()
        for slot in range(1, 8):
            col_copy(slot, piece).wait_send()
        for slot in range(8):
            pair_copy(slot, piece).wait_send()
    total = landed[0]
    for at in range(15, 0, -1):
        share_copy(at).wait_recv()
        total = total + landed[at]
    square_buf[0:FRAMES, :] = total / total[:, 64:65]
    out_ref[...] = square_buf[...].T[0:64, 0:FRAMES]
    for at in range(1, 16):
        share_copy(at).wait_send()


def per_device(row_frames, col_frames, vectors):
    vmem = pl.BlockSpec(memory_space=pltpu.VMEM)
    dma = pltpu.SemaphoreType.DMA
    return pl.pallas_call(
        body,
        name="qcp_product",
        out_shape=jax.ShapeDtypeStruct(vectors.shape, jnp.float32),
        in_specs=[pl.BlockSpec(memory_space=pl.ANY)] * 3,
        out_specs=vmem,
        scratch_shapes=[
            pltpu.VMEM(row_frames.shape, jnp.float32),
            pltpu.VMEM(col_frames.shape, jnp.float32),
            pltpu.VMEM(vectors.shape, jnp.float32),
            pltpu.VMEM((16, 96, ATOMS), jnp.float32),
            pltpu.VMEM((2, 8, 112, ATOMS), jnp.float32),
            pltpu.VMEM((4, 384, 768), jnp.bfloat16),
            pltpu.VMEM((4, 384, 768), jnp.bfloat16),
            pltpu.VMEM((4, 384, 128), jnp.bfloat16),
            pltpu.VMEM((4, 128, 128), jnp.float32),
            pltpu.VMEM((4, 8, 128), jnp.float32),
            pltpu.VMEM((384, 384), jnp.float32),
            pltpu.VMEM((384, 384), jnp.float32),
            pltpu.VMEM((128, 384), jnp.bfloat16),
            pltpu.VMEM((128, 384), jnp.bfloat16),
            pltpu.VMEM((4, 128, 128), jnp.float32),
            pltpu.VMEM((16, FRAMES, 128), jnp.float32),
            pltpu.VMEM((16, FRAMES, 128), jnp.float32),
            pltpu.VMEM((128, 128), jnp.float32),
            dma((3,)), dma((16, 3)), dma((16, 3)), dma((8, 3)), dma((8, 3)),
            dma((8, 3)), dma((8, 3)), dma((16,)), dma((16,)),
        ],
        compiler_params=pltpu.CompilerParams(
            collective_id=0, has_side_effects=True, vmem_limit_bytes=40 << 20,
        ),
    )(row_frames, col_frames, vectors)


def solution(mesh):
    return jax.shard_map(
        per_device,
        mesh=mesh,
        in_specs=(
            P(None, ("row", "col"), None),
            P(None, ("col", "row"), None),
            P(None, ("col", "row")),
        ),
        out_specs=P(None, ("row", "col")),
        check_vma=False,
    )
```

```python
import jax
import jax.numpy as jnp
from jax import lax
from jax.experimental import pallas as pl
from jax.experimental.pallas import tpu as pltpu
from jax.sharding import PartitionSpec as P

NEWTON = 8
ATOMS = 256
FRAMES = 32
SLICE = 32
MESH = pl.DeviceIdType.MESH

ROW_SLOTS = (
    (0, 0), (1, 0), (3, 0), (0, 1),
    (0, 3), (1, 1), (1, 3), (2, 0),
    (3, 1), (3, 3), (0, 2), (2, 1),
    (2, 3), (1, 2), (3, 2), (2, 2),
)
ROW_AT = {where: at for at, where in enumerate(ROW_SLOTS)}
COL_GROUPS = ((1, 7), (2, 6), (3, 5), (0, 4))


def row_source(slot):
    first, second = slot
    if second == 0:
        source = {1: (0, 0), 3: (0, 0), 2: (1, 0)}[first]
        return source, ((3, 0) if first in (1, 2) else (1, 0))
    if second == 1:
        return (first, 0), (0, 3)
    if second == 3:
        return (first, 0), (0, 1)
    if first < 2:
        return (first, 1), (0, 3)
    return (first, 3), (0, 1)


def split(value):
    high = value.astype(jnp.bfloat16)
    low = (value - high.astype(jnp.float32)).astype(jnp.bfloat16)
    return high, low


def kernel_values(moment, row_norm, col_norm):
    s00, s01, s02, s10, s11, s12, s20, s21, s22 = moment
    g00 = s00 * s00 + s10 * s10 + s20 * s20
    g11 = s01 * s01 + s11 * s11 + s21 * s21
    g22 = s02 * s02 + s12 * s12 + s22 * s22
    g01 = s00 * s01 + s10 * s11 + s20 * s21
    g02 = s00 * s02 + s10 * s12 + s20 * s22
    g12 = s01 * s02 + s11 * s12 + s21 * s22
    pair = g11 + g22
    trace = g00 + pair
    minors = g00 * pair + g11 * g22 - (g01 * g01 + g02 * g02 + g12 * g12)
    det = s00 * (s11 * s22 - s12 * s21) + s01 * (s12 * s20 - s10 * s22) + s02 * (s10 * s21 - s11 * s20)
    half_trace = 0.5 * trace
    free = half_trace * half_trace - minors
    det_two = det + det
    full_norm = row_norm + col_norm
    eigen = full_norm
    for _ in range(NEWTON):
        square = eigen * eigen
        upper = (0.75 * square - half_trace) * square - free
        lower = (square - trace) * eigen - det_two
        eigen = upper / lower
    return jnp.exp(jnp.minimum((eigen - full_norm) * (0.5 / ATOMS), 0.0))


ROW_PIECES = ((0, 32), (32, 32), (64, 32))
COL_PIECES = ((0, 32), (32, 32), (64, 48))
UNITS = (
    ((0, 0),),
    ((0, 1), (1, 1), (1, 0)),
    ((0, 2), (1, 2), (2, 2), (2, 1), (2, 0)),
    ((3, 0), (3, 1), (3, 2), (3, 3), (2, 3), (1, 3), (0, 3)),
)


def body(
    rows_hbm, cols_hbm, vec_hbm, out_ref,
    rows_ref, cols_ref, vec_ref,
    rbuf, cbuf, rsplit, csplit, vsplit, rnorm, cnorm, moments_a, moments_b, ksplit_a, ksplit_b,
    acc, parts, landed, square_buf,
    isem, rsend, rrecv, csend, crecv, psend, precv, ssend, srecv,
):
    row, col = lax.axis_index("row"), lax.axis_index("col")
    core = lax.rem(row, 2)
    at_x = lax.rem(lax.div(row, 2), 4)
    at_y = lax.rem(col, 2) * 2 + lax.div(row, 8)
    at_z = lax.div(col, 2)

    def device(first, second, along=0, other=False):
        to_x = lax.rem(at_x + (1 - core) * first + core * (4 - second), 4)
        to_y = lax.rem(at_y + (1 - core) * second + core * (4 - first), 4)
        to_z = lax.rem(at_z + (1 - core) * along + core * (8 - along), 8)
        to_core = 1 - core if other else core
        to_row = (lax.rem(to_y, 2) * 4 + to_x) * 2 + to_core
        return (to_row, to_z * 2 + lax.div(to_y, 2))

    neighbours = (
        device(1, 0), device(3, 0), device(0, 1), device(0, 3),
        device(0, 0, 1), device(0, 0, 7), device(0, 0, 0, True),
    )
    barrier = pltpu.get_barrier_semaphore()
    for neighbour in neighbours:
        pl.semaphore_signal(barrier, inc=1, device_id=neighbour, device_id_type=MESH)
    loads = (
        pltpu.make_async_copy(rows_hbm, rows_ref, isem.at[0]),
        pltpu.make_async_copy(cols_hbm, cols_ref, isem.at[1]),
        pltpu.make_async_copy(vec_hbm, vec_ref, isem.at[2]),
    )
    for load in loads:
        load.start()

    def row_copy(slot, piece):
        source, toward = row_source(slot)
        at, span = ROW_AT[slot], pl.ds(*ROW_PIECES[piece])
        return pltpu.make_async_remote_copy(
            src_ref=rbuf.at[ROW_AT[source], span], dst_ref=rbuf.at[at, span],
            send_sem=rsend.at[at, piece], recv_sem=rrecv.at[at, piece],
            device_id=device(*toward), device_id_type=MESH,
        )

    def col_copy(slot, piece):
        source, toward = (slot - 1, 7) if slot <= 4 else ((slot + 1) % 8, 1)
        span = pl.ds(*COL_PIECES[piece])
        return pltpu.make_async_remote_copy(
            src_ref=cbuf.at[0, source, span], dst_ref=cbuf.at[0, slot, span],
            send_sem=csend.at[slot, piece], recv_sem=crecv.at[slot, piece],
            device_id=device(0, 0, toward), device_id_type=MESH,
        )

    def pair_copy(slot, piece):
        span = pl.ds(*COL_PIECES[piece])
        return pltpu.make_async_remote_copy(
            src_ref=cbuf.at[0, slot, span], dst_ref=cbuf.at[1, slot, span],
            send_sem=psend.at[slot, piece], recv_sem=precv.at[slot, piece],
            device_id=device(0, 0, 0, True), device_id_type=MESH,
        )

    def share_copy(at):
        return pltpu.make_async_remote_copy(
            src_ref=parts.at[at], dst_ref=landed.at[at],
            send_sem=ssend.at[at], recv_sem=srecv.at[at],
            device_id=device(*ROW_SLOTS[at]), device_id_type=MESH,
        )

    loads[0].wait()
    for comp in range(3):
        frames = rows_ref[comp]
        centred = frames - jnp.mean(frames, axis=1, keepdims=True)
        rbuf[0, comp * FRAMES:(comp + 1) * FRAMES, :] = centred + centred
    loads[1].wait()
    for comp in range(3):
        frames = cols_ref[comp]
        cbuf[0, 0, comp * FRAMES:(comp + 1) * FRAMES, :] = frames - jnp.mean(frames, axis=1, keepdims=True)
    loads[2].wait()
    ones = jnp.ones((16, 64), jnp.float32)
    cbuf[0, 0, 96:112, :] = jnp.concatenate([vec_ref[0:16, :], ones, vec_ref[16:32, :], ones], axis=1)

    pl.semaphore_wait(barrier, len(neighbours))

    for piece in range(3):
        for slot in ((1, 0), (3, 0), (0, 1), (0, 3)):
            row_copy(slot, piece).start()
        col_copy(1, piece).start()
        col_copy(7, piece).start()
        pair_copy(0, piece).start()

    def pass_on(piece, cols, rows):
        for slot, onward in cols:
            col_copy(slot, piece).wait_recv()
            if onward is not None:
                col_copy(onward, piece).start()
            pair_copy(slot, piece).start()
        for slot, onward in rows:
            row_copy(slot, piece).wait_recv()
            for later in onward:
                row_copy(later, piece).start()

    def first_round(piece):
        pass_on(piece, ((1, 2), (7, 6)), (
            ((1, 0), ((2, 0), (1, 1), (1, 3))), ((3, 0), ((3, 1), (3, 3))), ((0, 1), ((0, 2),)),
        ))

    def second_round(piece):
        pass_on(piece, ((2, 3), (6, 5)), (
            ((2, 0), ((2, 1), (2, 3))), ((1, 1), ((1, 2),)), ((3, 3), ((3, 2),)),
        ))

    def third_round(piece):
        pass_on(piece, ((3, 4), (5, None)), (((2, 3), ((2, 2),)),))

    def settle(rows, cols):
        for piece in range(3):
            for slot in rows:
                row_copy(slot, piece).wait_recv()
            for slot in cols:
                pair_copy(slot, piece).wait_recv()

    def prepare_rows(chunk):
        for place in range(4):
            norm = jnp.zeros((FRAMES, 1), jnp.float32)
            for comp in range(3):
                value = rbuf[4 * chunk + place, comp * FRAMES:(comp + 1) * FRAMES, :]
                norm = norm + jnp.sum(value * value, axis=1, keepdims=True)
                high, low = split(value)
                at = pl.ds(comp * 128 + place * FRAMES, FRAMES)
                rsplit[chunk, at, 0:256] = high
                rsplit[chunk, at, 256:512] = high
                rsplit[chunk, at, 512:768] = low
            rnorm[chunk, place * FRAMES:(place + 1) * FRAMES, :] = jnp.broadcast_to(0.25 * norm, (FRAMES, 128))

    def prepare_cols(group):
        for place in range(4):
            kind, slot = place // 2, COL_GROUPS[group][place % 2]
            norm = jnp.zeros((FRAMES, 1), jnp.float32)
            for comp in range(3):
                value = cbuf[kind, slot, comp * FRAMES:(comp + 1) * FRAMES, :]
                norm = norm + jnp.sum(value * value, axis=1, keepdims=True)
                high, low = split(value)
                at = pl.ds(comp * 128 + place * FRAMES, FRAMES)
                csplit[group, at, 0:256] = high
                csplit[group, at, 256:512] = low
                csplit[group, at, 512:768] = high
            square_buf[place * FRAMES:(place + 1) * FRAMES, :] = jnp.broadcast_to(norm, (FRAMES, 128))
            for half in range(2):
                value = cbuf[kind, slot, 96:112, half * 128:(half + 1) * 128]
                high, low = split(value)
                start = place * FRAMES + half * 16
                vsplit[group, start:start + 16, :] = high
                vsplit[group, 128 + start:128 + start + 16, :] = high
                vsplit[group, 256 + start:256 + start + 16, :] = low
        cnorm[group] = square_buf[...].T[0:8, :]

    def share(chunk):
        for place in range(4):
            at = 4 * chunk + place
            value = acc[chunk, place * FRAMES:(place + 1) * FRAMES, :]
            if at == 0:
                landed[0] = value
            else:
                parts[at] = value
                share_copy(at).start()

    moments, ksplit = (moments_a, moments_b), (ksplit_a, ksplit_b)
    started, flight = set(), {"moments": None, "values": None, "count": 0}

    def advance(unit):
        count = flight["count"]
        if unit is not None:
            moments[count % 2][...] = lax.dot_general(
                rsplit[unit[0]], csplit[unit[1]], (((1,), (1,)), ((), ())),
                preferred_element_type=jnp.float32,
            )
        valued = flight["values"]
        if valued is not None:
            chunk, group = valued
            added = jnp.dot(ksplit[count % 2][...], vsplit[group], preferred_element_type=jnp.float32)
            acc[chunk] = acc[chunk] + added if chunk in started else added
            started.add(chunk)
        ready = flight["moments"]
        if ready is not None:
            chunk, group = ready
            held, into = moments[(count + 1) % 2], ksplit[(count + 1) % 2]
            col_norm = cnorm[group][0:1, :]
            for start in range(0, 128, SLICE):
                moment = [
                    held[first * 128 + start:first * 128 + start + SLICE, second * 128:(second + 1) * 128]
                    for first in range(3) for second in range(3)
                ]
                values = kernel_values(moment, rnorm[chunk, start:start + SLICE, :], col_norm)
                high, low = split(values)
                into[start:start + SLICE, 0:128] = high
                into[start:start + SLICE, 128:256] = low
                into[start:start + SLICE, 256:384] = high
        if valued is not None and valued[1] == 3:
            share(valued[0])
        flight["moments"], flight["values"], flight["count"] = unit, ready, count + 1

    for piece in range(3):
        first_round(piece)
    settle((), (1, 7))
    prepare_rows(0)
    prepare_cols(0)
    second_round(0)
    advance(UNITS[0][0])
    second_round(1)
    second_round(2)
    settle(((0, 3), (1, 3)), (2, 6))
    prepare_rows(1)
    prepare_cols(1)
    for piece in range(3):
        advance(UNITS[1][piece])
        third_round(piece)
    settle(((3, 1), (0, 2), (2, 1)), (3, 5))
    prepare_rows(2)
    prepare_cols(2)
    for at, unit in enumerate(UNITS[2]):
        advance(unit)
        if 1 <= at <= 3:
            col_copy(4, at - 1).wait_recv()
            pair_copy(4, at - 1).start()
    settle(((1, 2), (3, 2), (2, 2)), (0, 4))
    prepare_rows(3)
    prepare_cols(3)
    for unit in UNITS[3]:
        advance(unit)
    advance(None)
    advance(None)

    for piece in range(3):
        for slot in ROW_SLOTS[1:]:
            row_copy(slot, piece).wait_send()
        for slot in range(1, 8):
            col_copy(slot, piece).wait_send()
        for slot in range(8):
            pair_copy(slot, piece).wait_send()
    total = landed[0]
    for at in range(15, 0, -1):
        share_copy(at).wait_recv()
        total = total + landed[at]
    out_ref[...] = (total / total[:, 64:65])[:, 0:64]
    for at in range(1, 16):
        share_copy(at).wait_send()


def per_device(row_frames, col_frames, vectors):
    vmem = pl.BlockSpec(memory_space=pltpu.VMEM)
    dma = pltpu.SemaphoreType.DMA
    return pl.pallas_call(
        body,
        name="qcp_product",
        out_shape=jax.ShapeDtypeStruct(vectors.shape[::-1], jnp.float32),
        in_specs=[pl.BlockSpec(memory_space=pltpu.HBM)] * 3,
        out_specs=vmem,
        scratch_shapes=[
            pltpu.VMEM(row_frames.shape, jnp.float32),
            pltpu.VMEM(col_frames.shape, jnp.float32),
            pltpu.VMEM(vectors.shape[::-1], jnp.float32),
            pltpu.VMEM((16, 96, ATOMS), jnp.float32),
            pltpu.VMEM((2, 8, 112, ATOMS), jnp.float32),
            pltpu.VMEM((4, 384, 768), jnp.bfloat16),
            pltpu.VMEM((4, 384, 768), jnp.bfloat16),
            pltpu.VMEM((4, 384, 128), jnp.bfloat16),
            pltpu.VMEM((4, 128, 128), jnp.float32),
            pltpu.VMEM((4, 8, 128), jnp.float32),
            pltpu.VMEM((384, 384), jnp.float32),
            pltpu.VMEM((384, 384), jnp.float32),
            pltpu.VMEM((128, 384), jnp.bfloat16),
            pltpu.VMEM((128, 384), jnp.bfloat16),
            pltpu.VMEM((4, 128, 128), jnp.float32),
            pltpu.VMEM((16, FRAMES, 128), jnp.float32),
            pltpu.VMEM((16, FRAMES, 128), jnp.float32),
            pltpu.VMEM((128, 128), jnp.float32),
            dma((3,)), dma((16, 3)), dma((16, 3)), dma((8, 3)), dma((8, 3)),
            dma((8, 3)), dma((8, 3)), dma((16,)), dma((16,)),
        ],
        compiler_params=pltpu.CompilerParams(
            collective_id=0, has_side_effects=True, vmem_limit_bytes=67043328,
        ),
    )(row_frames, col_frames, vectors.T).T


def solution(mesh):
    return jax.shard_map(
        per_device,
        mesh=mesh,
        in_specs=(
            P(None, ("row", "col"), None),
            P(None, ("col", "row"), None),
            P(None, ("col", "row")),
        ),
        out_specs=P(None, ("row", "col")),
        check_vma=False,
    )
```

```python
import jax
import jax.numpy as jnp
from jax import lax
from jax.experimental import pallas as pl
from jax.experimental.pallas import tpu as pltpu
from jax.sharding import PartitionSpec as P

NEWTON = 8
ATOMS = 256
FRAMES = 32
SLICE = 32
MESH = pl.DeviceIdType.MESH

ROW_SLOTS = (
    (0, 0), (1, 0), (3, 0), (0, 1),
    (0, 3), (1, 1), (1, 3), (2, 0),
    (3, 1), (3, 3), (0, 2), (2, 1),
    (2, 3), (1, 2), (3, 2), (2, 2),
)
ROW_AT = {where: at for at, where in enumerate(ROW_SLOTS)}
COL_GROUPS = ((1, 7), (2, 6), (3, 5), (0, 4))


def row_source(slot):
    first, second = slot
    if second == 0:
        source = {1: (0, 0), 3: (0, 0), 2: (1, 0)}[first]
        return source, ((3, 0) if first in (1, 2) else (1, 0))
    if second == 1:
        return (first, 0), (0, 3)
    if second == 3:
        return (first, 0), (0, 1)
    if first < 2:
        return (first, 1), (0, 3)
    return (first, 3), (0, 1)


def split(value):
    high = value.astype(jnp.bfloat16)
    low = (value - high.astype(jnp.float32)).astype(jnp.bfloat16)
    return high, low


def kernel_values(moment, row_norm, col_norm):
    s00, s01, s02, s10, s11, s12, s20, s21, s22 = moment
    g00 = s00 * s00 + s10 * s10 + s20 * s20
    g11 = s01 * s01 + s11 * s11 + s21 * s21
    g22 = s02 * s02 + s12 * s12 + s22 * s22
    g01 = s00 * s01 + s10 * s11 + s20 * s21
    g02 = s00 * s02 + s10 * s12 + s20 * s22
    g12 = s01 * s02 + s11 * s12 + s21 * s22
    pair = g11 + g22
    trace = g00 + pair
    minors = g00 * pair + g11 * g22 - (g01 * g01 + g02 * g02 + g12 * g12)
    det = s00 * (s11 * s22 - s12 * s21) + s01 * (s12 * s20 - s10 * s22) + s02 * (s10 * s21 - s11 * s20)
    half_trace = 0.5 * trace
    free = half_trace * half_trace - minors
    det_two = det + det
    full_norm = row_norm + col_norm
    eigen = full_norm
    for _ in range(NEWTON):
        square = eigen * eigen
        upper = (0.75 * square - half_trace) * square - free
        lower = (square - trace) * eigen - det_two
        eigen = upper / lower
    return jnp.exp(jnp.minimum((eigen - full_norm) * (0.5 / ATOMS), 0.0))


ROW_PIECES = ((0, 32), (32, 32), (64, 32))
COL_PIECES = ((0, 32), (32, 32), (64, 48))
UNITS = (
    ((0, 0),),
    ((1, 0), (1, 1), (0, 1)),
    ((2, 0), (2, 1), (2, 2), (1, 2), (0, 2)),
    ((3, 0), (3, 1), (3, 2), (3, 3), (2, 3), (1, 3), (0, 3)),
)


def body(
    rows_hbm, cols_hbm, vec_hbm, out_ref,
    rows_ref, cols_ref, vec_ref,
    rbuf, cbuf, rsplit, csplit, vsplit, rnorm, cnorm, moments_a, moments_b, ksplit_a, ksplit_b,
    acc, parts, landed, square_buf,
    isem, rsend, rrecv, csend, crecv, psend, precv, ssend, srecv,
):
    row, col = lax.axis_index("row"), lax.axis_index("col")
    core = lax.rem(row, 2)
    at_x = lax.rem(lax.div(row, 2), 4)
    at_y = lax.rem(col, 2) * 2 + lax.div(row, 8)
    at_z = lax.div(col, 2)

    def device(first, second, along=0, other=False):
        to_x = lax.rem(at_x + (1 - core) * first + core * (4 - second), 4)
        to_y = lax.rem(at_y + (1 - core) * second + core * (4 - first), 4)
        to_z = lax.rem(at_z + (1 - core) * along + core * (8 - along), 8)
        to_core = 1 - core if other else core
        to_row = (lax.rem(to_y, 2) * 4 + to_x) * 2 + to_core
        return (to_row, to_z * 2 + lax.div(to_y, 2))

    neighbours = (
        device(1, 0), device(3, 0), device(0, 1), device(0, 3),
        device(0, 0, 1), device(0, 0, 7), device(0, 0, 0, True),
    )
    barrier = pltpu.get_barrier_semaphore()
    for neighbour in neighbours:
        pl.semaphore_signal(barrier, inc=1, device_id=neighbour, device_id_type=MESH)
    loads = (
        pltpu.make_async_copy(rows_hbm, rows_ref, isem.at[0]),
        pltpu.make_async_copy(cols_hbm, cols_ref, isem.at[1]),
        pltpu.make_async_copy(vec_hbm, vec_ref, isem.at[2]),
    )
    for load in loads:
        load.start()

    def row_copy(slot, piece):
        source, toward = row_source(slot)
        at, span = ROW_AT[slot], pl.ds(*ROW_PIECES[piece])
        return pltpu.make_async_remote_copy(
            src_ref=rbuf.at[ROW_AT[source], span], dst_ref=rbuf.at[at, span],
            send_sem=rsend.at[at, piece], recv_sem=rrecv.at[at, piece],
            device_id=device(*toward), device_id_type=MESH,
        )

    def col_copy(slot, piece):
        source, toward = (slot - 1, 7) if slot <= 4 else ((slot + 1) % 8, 1)
        span = pl.ds(*COL_PIECES[piece])
        return pltpu.make_async_remote_copy(
            src_ref=cbuf.at[0, source, span], dst_ref=cbuf.at[0, slot, span],
            send_sem=csend.at[slot, piece], recv_sem=crecv.at[slot, piece],
            device_id=device(0, 0, toward), device_id_type=MESH,
        )

    def pair_copy(slot, piece):
        span = pl.ds(*COL_PIECES[piece])
        return pltpu.make_async_remote_copy(
            src_ref=cbuf.at[0, slot, span], dst_ref=cbuf.at[1, slot, span],
            send_sem=psend.at[slot, piece], recv_sem=precv.at[slot, piece],
            device_id=device(0, 0, 0, True), device_id_type=MESH,
        )

    def share_copy(at):
        return pltpu.make_async_remote_copy(
            src_ref=parts.at[at], dst_ref=landed.at[at],
            send_sem=ssend.at[at], recv_sem=srecv.at[at],
            device_id=device(*ROW_SLOTS[at]), device_id_type=MESH,
        )

    loads[0].wait()
    for comp in range(3):
        frames = rows_ref[comp]
        centred = frames - jnp.mean(frames, axis=1, keepdims=True)
        rbuf[0, comp * FRAMES:(comp + 1) * FRAMES, :] = centred + centred
    loads[1].wait()
    for comp in range(3):
        frames = cols_ref[comp]
        cbuf[0, 0, comp * FRAMES:(comp + 1) * FRAMES, :] = frames - jnp.mean(frames, axis=1, keepdims=True)
    loads[2].wait()
    ones = jnp.ones((16, 64), jnp.float32)
    cbuf[0, 0, 96:112, :] = jnp.concatenate([vec_ref[0:16, :], ones, vec_ref[16:32, :], ones], axis=1)

    pl.semaphore_wait(barrier, len(neighbours))

    for piece in range(3):
        for slot in ((1, 0), (3, 0), (0, 1), (0, 3)):
            row_copy(slot, piece).start()
        col_copy(1, piece).start()
        col_copy(7, piece).start()
        pair_copy(0, piece).start()

    def pass_on(piece, cols, rows):
        for slot, onward in cols:
            col_copy(slot, piece).wait_recv()
            if onward is not None:
                col_copy(onward, piece).start()
            pair_copy(slot, piece).start()
        for slot, onward in rows:
            row_copy(slot, piece).wait_recv()
            for later in onward:
                row_copy(later, piece).start()

    def first_round(piece):
        pass_on(piece, ((1, 2), (7, 6)), (
            ((1, 0), ((2, 0), (1, 1), (1, 3))), ((3, 0), ((3, 1), (3, 3))), ((0, 1), ((0, 2),)),
        ))

    def second_round(piece):
        pass_on(piece, ((2, 3), (6, 5)), (
            ((2, 0), ((2, 1), (2, 3))), ((1, 1), ((1, 2),)), ((3, 3), ((3, 2),)),
        ))

    def third_round(piece):
        pass_on(piece, ((3, 4), (5, None)), (((2, 3), ((2, 2),)),))

    def settle(rows, cols):
        for piece in range(3):
            for slot in rows:
                row_copy(slot, piece).wait_recv()
            for slot in cols:
                pair_copy(slot, piece).wait_recv()

    def prepare_rows(chunk):
        for place in range(4):
            norm = jnp.zeros((FRAMES, 1), jnp.float32)
            for comp in range(3):
                value = rbuf[4 * chunk + place, comp * FRAMES:(comp + 1) * FRAMES, :]
                norm = norm + jnp.sum(value * value, axis=1, keepdims=True)
                high, low = split(value)
                at = pl.ds(comp * 128 + place * FRAMES, FRAMES)
                rsplit[chunk, at, 0:256] = high
                rsplit[chunk, at, 256:512] = high
                rsplit[chunk, at, 512:768] = low
            rnorm[chunk, place * FRAMES:(place + 1) * FRAMES, :] = jnp.broadcast_to(0.25 * norm, (FRAMES, 128))

    def prepare_cols(group):
        for place in range(4):
            kind, slot = place // 2, COL_GROUPS[group][place % 2]
            norm = jnp.zeros((FRAMES, 1), jnp.float32)
            for comp in range(3):
                value = cbuf[kind, slot, comp * FRAMES:(comp + 1) * FRAMES, :]
                norm = norm + jnp.sum(value * value, axis=1, keepdims=True)
                high, low = split(value)
                at = pl.ds(comp * 128 + place * FRAMES, FRAMES)
                csplit[group, at, 0:256] = high
                csplit[group, at, 256:512] = low
                csplit[group, at, 512:768] = high
            square_buf[place * FRAMES:(place + 1) * FRAMES, :] = jnp.broadcast_to(norm, (FRAMES, 128))
            for half in range(2):
                value = cbuf[kind, slot, 96:112, half * 128:(half + 1) * 128]
                high, low = split(value)
                start = place * FRAMES + half * 16
                vsplit[group, start:start + 16, :] = high
                vsplit[group, 128 + start:128 + start + 16, :] = high
                vsplit[group, 256 + start:256 + start + 16, :] = low
        cnorm[group] = square_buf[...].T[0:8, :]

    def share(chunk):
        for place in range(4):
            at = 4 * chunk + place
            value = acc[chunk, place * FRAMES:(place + 1) * FRAMES, :]
            if at == 0:
                landed[0] = value
            else:
                parts[at] = value
                share_copy(at).start()

    moments, ksplit = (moments_a, moments_b), (ksplit_a, ksplit_b)
    started, flight = set(), {"moments": None, "values": None, "count": 0}

    def advance(unit):
        count = flight["count"]
        if unit is not None:
            moments[count % 2][...] = lax.dot_general(
                rsplit[unit[0]], csplit[unit[1]], (((1,), (1,)), ((), ())),
                preferred_element_type=jnp.float32,
            )
        valued = flight["values"]
        if valued is not None:
            chunk, group = valued
            added = jnp.dot(ksplit[count % 2][...], vsplit[group], preferred_element_type=jnp.float32)
            acc[chunk] = acc[chunk] + added if chunk in started else added
            started.add(chunk)
        ready = flight["moments"]
        if ready is not None:
            chunk, group = ready
            held, into = moments[(count + 1) % 2], ksplit[(count + 1) % 2]
            col_norm = cnorm[group][0:1, :]
            for start in range(0, 128, SLICE):
                moment = [
                    held[first * 128 + start:first * 128 + start + SLICE, second * 128:(second + 1) * 128]
                    for first in range(3) for second in range(3)
                ]
                values = kernel_values(moment, rnorm[chunk, start:start + SLICE, :], col_norm)
                high, low = split(values)
                into[start:start + SLICE, 0:128] = high
                into[start:start + SLICE, 128:256] = low
                into[start:start + SLICE, 256:384] = high
        if valued is not None and valued[1] == 3:
            share(valued[0])
        flight["moments"], flight["values"], flight["count"] = unit, ready, count + 1

    for piece in range(3):
        first_round(piece)
    settle((), (1, 7))
    prepare_rows(0)
    prepare_cols(0)
    second_round(0)
    advance(UNITS[0][0])
    second_round(1)
    second_round(2)
    settle(((0, 3), (1, 3)), ())
    prepare_rows(1)
    advance(UNITS[1][0])
    third_round(0)
    settle((), (2, 6))
    prepare_cols(1)
    advance(UNITS[1][1])
    third_round(1)
    advance(UNITS[1][2])
    third_round(2)
    settle(((3, 1), (0, 2), (2, 1)), ())
    prepare_rows(2)
    for at, unit in enumerate(UNITS[2]):
        if at == 2:
            settle((), (3, 5))
            prepare_cols(2)
        advance(unit)
        if 1 <= at <= 3:
            col_copy(4, at - 1).wait_recv()
            pair_copy(4, at - 1).start()
    settle(((1, 2), (3, 2), (2, 2)), ())
    prepare_rows(3)
    for at, unit in enumerate(UNITS[3]):
        if at == 3:
            settle((), (0, 4))
            prepare_cols(3)
        advance(unit)
    advance(None)
    advance(None)

    for piece in range(3):
        for slot in ROW_SLOTS[1:]:
            row_copy(slot, piece).wait_send()
        for slot in range(1, 8):
            col_copy(slot, piece).wait_send()
        for slot in range(8):
            pair_copy(slot, piece).wait_send()
    total = landed[0]
    for at in range(15, 0, -1):
        share_copy(at).wait_recv()
        total = total + landed[at]
    out_ref[...] = (total / total[:, 64:65])[:, 0:64]
    for at in range(1, 16):
        share_copy(at).wait_send()


def per_device(row_frames, col_frames, vectors):
    vmem = pl.BlockSpec(memory_space=pltpu.VMEM)
    dma = pltpu.SemaphoreType.DMA
    return pl.pallas_call(
        body,
        name="qcp_product",
        out_shape=jax.ShapeDtypeStruct(vectors.shape[::-1], jnp.float32),
        in_specs=[pl.BlockSpec(memory_space=pltpu.HBM)] * 3,
        out_specs=vmem,
        scratch_shapes=[
            pltpu.VMEM(row_frames.shape, jnp.float32),
            pltpu.VMEM(col_frames.shape, jnp.float32),
            pltpu.VMEM(vectors.shape[::-1], jnp.float32),
            pltpu.VMEM((16, 96, ATOMS), jnp.float32),
            pltpu.VMEM((2, 8, 112, ATOMS), jnp.float32),
            pltpu.VMEM((4, 384, 768), jnp.bfloat16),
            pltpu.VMEM((4, 384, 768), jnp.bfloat16),
            pltpu.VMEM((4, 384, 128), jnp.bfloat16),
            pltpu.VMEM((4, 128, 128), jnp.float32),
            pltpu.VMEM((4, 8, 128), jnp.float32),
            pltpu.VMEM((384, 384), jnp.float32),
            pltpu.VMEM((384, 384), jnp.float32),
            pltpu.VMEM((128, 384), jnp.bfloat16),
            pltpu.VMEM((128, 384), jnp.bfloat16),
            pltpu.VMEM((4, 128, 128), jnp.float32),
            pltpu.VMEM((16, FRAMES, 128), jnp.float32),
            pltpu.VMEM((16, FRAMES, 128), jnp.float32),
            pltpu.VMEM((128, 128), jnp.float32),
            dma((3,)), dma((16, 3)), dma((16, 3)), dma((8, 3)), dma((8, 3)),
            dma((8, 3)), dma((8, 3)), dma((16,)), dma((16,)),
        ],
        compiler_params=pltpu.CompilerParams(
            collective_id=0, has_side_effects=True, vmem_limit_bytes=67043328,
        ),
    )(row_frames, col_frames, vectors.T).T


def solution(mesh):
    return jax.shard_map(
        per_device,
        mesh=mesh,
        in_specs=(
            P(None, ("row", "col"), None),
            P(None, ("col", "row"), None),
            P(None, ("col", "row")),
        ),
        out_specs=P(None, ("row", "col")),
        check_vma=False,
    )
```

```python
import jax
import jax.numpy as jnp
from jax import lax
from jax.experimental import pallas as pl
from jax.experimental.pallas import tpu as pltpu
from jax.sharding import PartitionSpec as P

NEWTON = 8
ATOMS = 256
FRAMES = 32
SLICE = 32
MESH = pl.DeviceIdType.MESH

ROW_SLOTS = (
    (0, 0), (1, 0), (3, 0), (0, 1),
    (0, 3), (1, 1), (1, 3), (2, 0),
    (3, 1), (3, 3), (0, 2), (2, 1),
    (2, 3), (1, 2), (3, 2), (2, 2),
)
ROW_AT = {where: at for at, where in enumerate(ROW_SLOTS)}
COL_GROUPS = ((1, 7), (2, 6), (3, 5), (0, 4))


def row_source(slot):
    first, second = slot
    if second == 0:
        source = {1: (0, 0), 3: (0, 0), 2: (1, 0)}[first]
        return source, ((3, 0) if first in (1, 2) else (1, 0))
    if second == 1:
        return (first, 0), (0, 3)
    if second == 3:
        return (first, 0), (0, 1)
    if first < 2:
        return (first, 1), (0, 3)
    return (first, 3), (0, 1)


def split(value):
    high = value.astype(jnp.bfloat16)
    low = (value - high.astype(jnp.float32)).astype(jnp.bfloat16)
    return high, low


def kernel_values(moment, row_norm, col_norm):
    s00, s01, s02, s10, s11, s12, s20, s21, s22 = moment
    g00 = s00 * s00 + s10 * s10 + s20 * s20
    g11 = s01 * s01 + s11 * s11 + s21 * s21
    g22 = s02 * s02 + s12 * s12 + s22 * s22
    g01 = s00 * s01 + s10 * s11 + s20 * s21
    g02 = s00 * s02 + s10 * s12 + s20 * s22
    g12 = s01 * s02 + s11 * s12 + s21 * s22
    pair = g11 + g22
    trace = g00 + pair
    minors = g00 * pair + g11 * g22 - (g01 * g01 + g02 * g02 + g12 * g12)
    det = s00 * (s11 * s22 - s12 * s21) + s01 * (s12 * s20 - s10 * s22) + s02 * (s10 * s21 - s11 * s20)
    half_trace = 0.5 * trace
    free = half_trace * half_trace - minors
    det_two = det + det
    full_norm = row_norm + col_norm
    eigen = full_norm
    for _ in range(NEWTON):
        square = eigen * eigen
        upper = (0.75 * square - half_trace) * square - free
        lower = (square - trace) * eigen - det_two
        eigen = upper / lower
    return jnp.exp(jnp.minimum((eigen - full_norm) * (0.5 / ATOMS), 0.0))


ROW_PIECES = ((0, 48), (48, 48))
COL_PIECES = ((0, 56), (56, 56))
UNITS = (
    ((0, 0),),
    ((1, 0), (1, 1), (0, 1)),
    ((2, 0), (2, 1), (2, 2), (1, 2), (0, 2)),
    ((3, 0), (3, 1), (3, 2), (3, 3), (2, 3), (1, 3), (0, 3)),
)


def body(
    rows_hbm, cols_hbm, vec_hbm, out_ref,
    rows_ref, cols_ref, vec_ref,
    rbuf, cbuf, rsplit, csplit, vsplit, rnorm, cnorm, moments_a, moments_b, ksplit_a, ksplit_b,
    acc, parts, landed, square_buf,
    isem, rsend, rrecv, csend, crecv, psend, precv, ssend, srecv,
):
    row, col = lax.axis_index("row"), lax.axis_index("col")
    core = lax.rem(row, 2)
    at_x = lax.rem(lax.div(row, 2), 4)
    at_y = lax.rem(col, 2) * 2 + lax.div(row, 8)
    at_z = lax.div(col, 2)

    def device(first, second, along=0, other=False):
        to_x = lax.rem(at_x + (1 - core) * first + core * (4 - second), 4)
        to_y = lax.rem(at_y + (1 - core) * second + core * (4 - first), 4)
        to_z = lax.rem(at_z + (1 - core) * along + core * (8 - along), 8)
        to_core = 1 - core if other else core
        to_row = (lax.rem(to_y, 2) * 4 + to_x) * 2 + to_core
        return (to_row, to_z * 2 + lax.div(to_y, 2))

    neighbours = (
        device(1, 0), device(3, 0), device(0, 1), device(0, 3),
        device(0, 0, 1), device(0, 0, 7), device(0, 0, 0, True),
    )
    barrier = pltpu.get_barrier_semaphore()
    for neighbour in neighbours:
        pl.semaphore_signal(barrier, inc=1, device_id=neighbour, device_id_type=MESH)
    loads = (
        pltpu.make_async_copy(rows_hbm, rows_ref, isem.at[0]),
        pltpu.make_async_copy(cols_hbm, cols_ref, isem.at[1]),
        pltpu.make_async_copy(vec_hbm, vec_ref, isem.at[2]),
    )
    for load in loads:
        load.start()

    def row_copy(slot, piece):
        source, toward = row_source(slot)
        at, span = ROW_AT[slot], pl.ds(*ROW_PIECES[piece])
        return pltpu.make_async_remote_copy(
            src_ref=rbuf.at[ROW_AT[source], span], dst_ref=rbuf.at[at, span],
            send_sem=rsend.at[at, piece], recv_sem=rrecv.at[at, piece],
            device_id=device(*toward), device_id_type=MESH,
        )

    def col_copy(slot, piece):
        source, toward = (slot - 1, 7) if slot <= 4 else ((slot + 1) % 8, 1)
        span = pl.ds(*COL_PIECES[piece])
        return pltpu.make_async_remote_copy(
            src_ref=cbuf.at[0, source, span], dst_ref=cbuf.at[0, slot, span],
            send_sem=csend.at[slot, piece], recv_sem=crecv.at[slot, piece],
            device_id=device(0, 0, toward), device_id_type=MESH,
        )

    def pair_copy(slot, piece):
        span = pl.ds(*COL_PIECES[piece])
        return pltpu.make_async_remote_copy(
            src_ref=cbuf.at[0, slot, span], dst_ref=cbuf.at[1, slot, span],
            send_sem=psend.at[slot, piece], recv_sem=precv.at[slot, piece],
            device_id=device(0, 0, 0, True), device_id_type=MESH,
        )

    def share_copy(at):
        return pltpu.make_async_remote_copy(
            src_ref=parts.at[at], dst_ref=landed.at[at],
            send_sem=ssend.at[at], recv_sem=srecv.at[at],
            device_id=device(*ROW_SLOTS[at]), device_id_type=MESH,
        )

    loads[0].wait()
    for comp in range(3):
        frames = rows_ref[comp]
        centred = frames - jnp.mean(frames, axis=1, keepdims=True)
        rbuf[0, comp * FRAMES:(comp + 1) * FRAMES, :] = centred + centred
    loads[1].wait()
    for comp in range(3):
        frames = cols_ref[comp]
        cbuf[0, 0, comp * FRAMES:(comp + 1) * FRAMES, :] = frames - jnp.mean(frames, axis=1, keepdims=True)
    loads[2].wait()
    ones = jnp.ones((16, 64), jnp.float32)
    cbuf[0, 0, 96:112, :] = jnp.concatenate([vec_ref[0:16, :], ones, vec_ref[16:32, :], ones], axis=1)

    pl.semaphore_wait(barrier, len(neighbours))

    for piece in range(2):
        for slot in ((1, 0), (3, 0), (0, 1), (0, 3)):
            row_copy(slot, piece).start()
        col_copy(1, piece).start()
        col_copy(7, piece).start()
        pair_copy(0, piece).start()

    def pass_on(piece, cols, rows):
        for slot, onward in cols:
            col_copy(slot, piece).wait_recv()
            if onward is not None:
                col_copy(onward, piece).start()
            pair_copy(slot, piece).start()
        for slot, onward in rows:
            row_copy(slot, piece).wait_recv()
            for later in onward:
                row_copy(later, piece).start()

    def first_round(piece):
        pass_on(piece, ((1, 2), (7, 6)), (
            ((1, 0), ((2, 0), (1, 1), (1, 3))), ((3, 0), ((3, 1), (3, 3))), ((0, 1), ((0, 2),)),
        ))

    def second_round(piece):
        pass_on(piece, ((2, 3), (6, 5)), (
            ((2, 0), ((2, 1), (2, 3))), ((1, 1), ((1, 2),)), ((3, 3), ((3, 2),)),
        ))

    def third_round(piece):
        pass_on(piece, ((3, 4), (5, None)), (((2, 3), ((2, 2),)),))

    def settle(rows, cols):
        for piece in range(2):
            for slot in rows:
                row_copy(slot, piece).wait_recv()
            for slot in cols:
                pair_copy(slot, piece).wait_recv()

    def prepare_rows(chunk):
        for place in range(4):
            norm = jnp.zeros((FRAMES, 1), jnp.float32)
            for comp in range(3):
                value = rbuf[4 * chunk + place, comp * FRAMES:(comp + 1) * FRAMES, :]
                norm = norm + jnp.sum(value * value, axis=1, keepdims=True)
                high, low = split(value)
                at = pl.ds(comp * 128 + place * FRAMES, FRAMES)
                rsplit[chunk, at, 0:256] = high
                rsplit[chunk, at, 256:512] = high
                rsplit[chunk, at, 512:768] = low
            rnorm[chunk, place * FRAMES:(place + 1) * FRAMES, :] = jnp.broadcast_to(0.25 * norm, (FRAMES, 128))

    def prepare_cols(group):
        for place in range(4):
            kind, slot = place // 2, COL_GROUPS[group][place % 2]
            norm = jnp.zeros((FRAMES, 1), jnp.float32)
            for comp in range(3):
                value = cbuf[kind, slot, comp * FRAMES:(comp + 1) * FRAMES, :]
                norm = norm + jnp.sum(value * value, axis=1, keepdims=True)
                high, low = split(value)
                at = pl.ds(comp * 128 + place * FRAMES, FRAMES)
                csplit[group, at, 0:256] = high
                csplit[group, at, 256:512] = low
                csplit[group, at, 512:768] = high
            square_buf[place * FRAMES:(place + 1) * FRAMES, :] = jnp.broadcast_to(norm, (FRAMES, 128))
            for half in range(2):
                value = cbuf[kind, slot, 96:112, half * 128:(half + 1) * 128]
                high, low = split(value)
                start = place * FRAMES + half * 16
                vsplit[group, start:start + 16, :] = high
                vsplit[group, 128 + start:128 + start + 16, :] = high
                vsplit[group, 256 + start:256 + start + 16, :] = low
        cnorm[group] = square_buf[...].T[0:8, :]

    def share(chunk):
        for place in range(4):
            at = 4 * chunk + place
            value = acc[chunk, place * FRAMES:(place + 1) * FRAMES, :]
            if at == 0:
                landed[0] = value
            else:
                parts[at] = value
                share_copy(at).start()

    moments, ksplit = (moments_a, moments_b), (ksplit_a, ksplit_b)
    started, flight = set(), {"moments": None, "values": None, "count": 0}

    def advance(unit):
        count = flight["count"]
        if unit is not None:
            moments[count % 2][...] = lax.dot_general(
                rsplit[unit[0]], csplit[unit[1]], (((1,), (1,)), ((), ())),
                preferred_element_type=jnp.float32,
            )
        valued = flight["values"]
        if valued is not None:
            chunk, group = valued
            added = jnp.dot(ksplit[count % 2][...], vsplit[group], preferred_element_type=jnp.float32)
            acc[chunk] = acc[chunk] + added if chunk in started else added
            started.add(chunk)
        ready = flight["moments"]
        if ready is not None:
            chunk, group = ready
            held, into = moments[(count + 1) % 2], ksplit[(count + 1) % 2]
            col_norm = cnorm[group][0:1, :]
            for start in range(0, 128, SLICE):
                moment = [
                    held[first * 128 + start:first * 128 + start + SLICE, second * 128:(second + 1) * 128]
                    for first in range(3) for second in range(3)
                ]
                values = kernel_values(moment, rnorm[chunk, start:start + SLICE, :], col_norm)
                high, low = split(values)
                into[start:start + SLICE, 0:128] = high
                into[start:start + SLICE, 128:256] = low
                into[start:start + SLICE, 256:384] = high
        if valued is not None and valued[1] == 3:
            share(valued[0])
        flight["moments"], flight["values"], flight["count"] = unit, ready, count + 1

    for piece in range(2):
        first_round(piece)
    settle((), (1, 7))
    prepare_rows(0)
    prepare_cols(0)
    second_round(0)
    advance(UNITS[0][0])
    second_round(1)
    settle(((0, 3), (1, 3)), ())
    prepare_rows(1)
    advance(UNITS[1][0])
    third_round(0)
    settle((), (2, 6))
    prepare_cols(1)
    advance(UNITS[1][1])
    third_round(1)
    advance(UNITS[1][2])
    settle(((3, 1), (0, 2), (2, 1)), ())
    prepare_rows(2)
    for at, unit in enumerate(UNITS[2]):
        if at == 2:
            settle((), (3, 5))
            prepare_cols(2)
        advance(unit)
        if 1 <= at <= 2:
            col_copy(4, at - 1).wait_recv()
            pair_copy(4, at - 1).start()
    settle(((1, 2), (3, 2), (2, 2)), ())
    prepare_rows(3)
    for at, unit in enumerate(UNITS[3]):
        if at == 3:
            settle((), (0, 4))
            prepare_cols(3)
        advance(unit)
    advance(None)
    advance(None)

    for piece in range(2):
        for slot in ROW_SLOTS[1:]:
            row_copy(slot, piece).wait_send()
        for slot in range(1, 8):
            col_copy(slot, piece).wait_send()
        for slot in range(8):
            pair_copy(slot, piece).wait_send()
    total = landed[0]
    for at in range(15, 0, -1):
        share_copy(at).wait_recv()
        total = total + landed[at]
    out_ref[...] = (total / total[:, 64:65])[:, 0:64]
    for at in range(1, 16):
        share_copy(at).wait_send()


def per_device(row_frames, col_frames, vectors):
    vmem = pl.BlockSpec(memory_space=pltpu.VMEM)
    dma = pltpu.SemaphoreType.DMA
    return pl.pallas_call(
        body,
        name="qcp_product",
        out_shape=jax.ShapeDtypeStruct(vectors.shape[::-1], jnp.float32),
        in_specs=[pl.BlockSpec(memory_space=pltpu.HBM)] * 3,
        out_specs=vmem,
        scratch_shapes=[
            pltpu.VMEM(row_frames.shape, jnp.float32),
            pltpu.VMEM(col_frames.shape, jnp.float32),
            pltpu.VMEM(vectors.shape[::-1], jnp.float32),
            pltpu.VMEM((16, 96, ATOMS), jnp.float32),
            pltpu.VMEM((2, 8, 112, ATOMS), jnp.float32),
            pltpu.VMEM((4, 384, 768), jnp.bfloat16),
            pltpu.VMEM((4, 384, 768), jnp.bfloat16),
            pltpu.VMEM((4, 384, 128), jnp.bfloat16),
            pltpu.VMEM((4, 128, 128), jnp.float32),
            pltpu.VMEM((4, 8, 128), jnp.float32),
            pltpu.VMEM((384, 384), jnp.float32),
            pltpu.VMEM((384, 384), jnp.float32),
            pltpu.VMEM((128, 384), jnp.bfloat16),
            pltpu.VMEM((128, 384), jnp.bfloat16),
            pltpu.VMEM((4, 128, 128), jnp.float32),
            pltpu.VMEM((16, FRAMES, 128), jnp.float32),
            pltpu.VMEM((16, FRAMES, 128), jnp.float32),
            pltpu.VMEM((128, 128), jnp.float32),
            dma((3,)), dma((16, 2)), dma((16, 2)), dma((8, 2)), dma((8, 2)),
            dma((8, 2)), dma((8, 2)), dma((16,)), dma((16,)),
        ],
        compiler_params=pltpu.CompilerParams(
            collective_id=0, has_side_effects=True, vmem_limit_bytes=67043328,
        ),
    )(row_frames, col_frames, vectors.T).T


def solution(mesh):
    return jax.shard_map(
        per_device,
        mesh=mesh,
        in_specs=(
            P(None, ("row", "col"), None),
            P(None, ("col", "row"), None),
            P(None, ("col", "row")),
        ),
        out_specs=P(None, ("row", "col")),
        check_vma=False,
    )
```

```python
import jax
import jax.numpy as jnp
from jax import lax
from jax.experimental import pallas as pl
from jax.experimental.pallas import tpu as pltpu
from jax.sharding import PartitionSpec as P

NEWTON = 8
ATOMS = 256
FRAMES = 32
SLICE = 32
MESH = pl.DeviceIdType.MESH

ROW_SLOTS = (
    (0, 0), (1, 0), (3, 0), (0, 1),
    (0, 3), (1, 1), (1, 3), (2, 0),
    (3, 1), (3, 3), (0, 2), (2, 1),
    (2, 3), (1, 2), (3, 2), (2, 2),
)
ROW_AT = {where: at for at, where in enumerate(ROW_SLOTS)}
COL_GROUPS = ((1, 7), (2, 6), (3, 5), (0, 4))


def row_source(slot):
    first, second = slot
    if second == 0:
        source = {1: (0, 0), 3: (0, 0), 2: (1, 0)}[first]
        return source, ((3, 0) if first in (1, 2) else (1, 0))
    if second == 1:
        return (first, 0), (0, 3)
    if second == 3:
        return (first, 0), (0, 1)
    if first < 2:
        return (first, 1), (0, 3)
    return (first, 3), (0, 1)


def split(value):
    high = value.astype(jnp.bfloat16)
    low = (value - high.astype(jnp.float32)).astype(jnp.bfloat16)
    return high, low


def kernel_values(moment, row_norm, col_norm):
    s00, s01, s02, s10, s11, s12, s20, s21, s22 = moment
    g00 = s00 * s00 + s10 * s10 + s20 * s20
    g11 = s01 * s01 + s11 * s11 + s21 * s21
    g22 = s02 * s02 + s12 * s12 + s22 * s22
    g01 = s00 * s01 + s10 * s11 + s20 * s21
    g02 = s00 * s02 + s10 * s12 + s20 * s22
    g12 = s01 * s02 + s11 * s12 + s21 * s22
    pair = g11 + g22
    trace = g00 + pair
    minors = g00 * pair + g11 * g22 - (g01 * g01 + g02 * g02 + g12 * g12)
    det = s00 * (s11 * s22 - s12 * s21) + s01 * (s12 * s20 - s10 * s22) + s02 * (s10 * s21 - s11 * s20)
    half_trace = 0.5 * trace
    free = half_trace * half_trace - minors
    det_two = det + det
    full_norm = row_norm + col_norm
    eigen = full_norm
    for _ in range(NEWTON):
        square = eigen * eigen
        upper = (0.75 * square - half_trace) * square - free
        lower = (square - trace) * eigen - det_two
        eigen = upper / lower
    return jnp.exp(jnp.minimum((eigen - full_norm) * (0.5 / ATOMS), 0.0))


ROW_PIECES = ((0, 48), (48, 48))
COL_PIECES = ((0, 56), (56, 56))
UNITS = (
    ((0, 0),),
    ((1, 0), (1, 1), (0, 1)),
    ((2, 0), (2, 1), (2, 2), (1, 2), (0, 2)),
    ((3, 0), (3, 1), (3, 2), (3, 3), (2, 3), (1, 3), (0, 3)),
)


def body(
    rows_hbm, cols_hbm, vec_hbm, out_ref,
    rows_ref, cols_ref, vec_ref,
    rbuf, cbuf, rsplit, csplit, vsplit, rnorm, cnorm, moments_a, moments_b, ksplit_a, ksplit_b,
    acc, parts, landed, square_buf,
    isem, rsend, rrecv, csend, crecv, psend, precv, ssend, srecv,
):
    row, col = lax.axis_index("row"), lax.axis_index("col")
    core = lax.rem(row, 2)
    at_x = lax.rem(lax.div(row, 2), 4)
    at_y = lax.rem(col, 2) * 2 + lax.div(row, 8)
    at_z = lax.div(col, 2)

    def device(first, second, along=0, other=False):
        to_x = lax.rem(at_x + (1 - core) * first + core * (4 - second), 4)
        to_y = lax.rem(at_y + (1 - core) * second + core * (4 - first), 4)
        to_z = lax.rem(at_z + (1 - core) * along + core * (8 - along), 8)
        to_core = 1 - core if other else core
        to_row = (lax.rem(to_y, 2) * 4 + to_x) * 2 + to_core
        return (to_row, to_z * 2 + lax.div(to_y, 2))

    neighbours = (
        device(1, 0), device(3, 0), device(0, 1), device(0, 3),
        device(0, 0, 1), device(0, 0, 7), device(0, 0, 0, True),
    )
    barrier = pltpu.get_barrier_semaphore()
    for neighbour in neighbours:
        pl.semaphore_signal(barrier, inc=1, device_id=neighbour, device_id_type=MESH)
    loads = (
        pltpu.make_async_copy(rows_hbm, rows_ref, isem.at[0]),
        pltpu.make_async_copy(cols_hbm, cols_ref, isem.at[1]),
        pltpu.make_async_copy(vec_hbm, vec_ref, isem.at[2]),
    )
    for load in loads:
        load.start()

    def row_copy(slot, piece):
        source, toward = row_source(slot)
        at, span = ROW_AT[slot], pl.ds(*ROW_PIECES[piece])
        return pltpu.make_async_remote_copy(
            src_ref=rbuf.at[ROW_AT[source], span], dst_ref=rbuf.at[at, span],
            send_sem=rsend.at[at, piece], recv_sem=rrecv.at[at, piece],
            device_id=device(*toward), device_id_type=MESH,
        )

    def col_copy(slot, piece):
        source, toward = (slot - 1, 7) if slot <= 4 else ((slot + 1) % 8, 1)
        span = pl.ds(*COL_PIECES[piece])
        return pltpu.make_async_remote_copy(
            src_ref=cbuf.at[0, source, span], dst_ref=cbuf.at[0, slot, span],
            send_sem=csend.at[slot, piece], recv_sem=crecv.at[slot, piece],
            device_id=device(0, 0, toward), device_id_type=MESH,
        )

    def pair_copy(slot, piece):
        span = pl.ds(*COL_PIECES[piece])
        return pltpu.make_async_remote_copy(
            src_ref=cbuf.at[0, slot, span], dst_ref=cbuf.at[1, slot, span],
            send_sem=psend.at[slot, piece], recv_sem=precv.at[slot, piece],
            device_id=device(0, 0, 0, True), device_id_type=MESH,
        )

    def share_copy(at):
        return pltpu.make_async_remote_copy(
            src_ref=parts.at[at], dst_ref=landed.at[at],
            send_sem=ssend.at[at], recv_sem=srecv.at[at],
            device_id=device(*ROW_SLOTS[at]), device_id_type=MESH,
        )

    loads[0].wait()
    for comp in range(3):
        frames = rows_ref[comp]
        centred = frames - jnp.mean(frames, axis=1, keepdims=True)
        rbuf[0, comp * FRAMES:(comp + 1) * FRAMES, :] = centred + centred
    loads[1].wait()
    for comp in range(3):
        frames = cols_ref[comp]
        cbuf[0, 0, comp * FRAMES:(comp + 1) * FRAMES, :] = frames - jnp.mean(frames, axis=1, keepdims=True)
    loads[2].wait()
    ones = jnp.ones((16, 64), jnp.float32)
    cbuf[0, 0, 96:112, :] = jnp.concatenate([vec_ref[0:16, :], ones, vec_ref[16:32, :], ones], axis=1)

    pl.semaphore_wait(barrier, len(neighbours))

    for piece in range(2):
        for slot in ((1, 0), (3, 0), (0, 1), (0, 3)):
            row_copy(slot, piece).start()
        col_copy(1, piece).start()
        col_copy(7, piece).start()
        pair_copy(0, piece).start()

    def pass_on(piece, cols, rows):
        for slot, onward in rows:
            row_copy(slot, piece).wait_recv()
            for later in onward:
                row_copy(later, piece).start()
        for slot, onward in cols:
            col_copy(slot, piece).wait_recv()
            if onward is not None:
                col_copy(onward, piece).start()
            pair_copy(slot, piece).start()

    def first_round(piece):
        pass_on(piece, ((1, 2), (7, 6)), (
            ((1, 0), ((2, 0), (1, 1), (1, 3))), ((3, 0), ((3, 1), (3, 3))), ((0, 1), ((0, 2),)),
        ))

    def second_round(piece):
        pass_on(piece, ((2, 3), (6, 5)), (
            ((2, 0), ((2, 1), (2, 3))), ((1, 1), ((1, 2),)), ((3, 3), ((3, 2),)),
        ))

    def third_round(piece):
        pass_on(piece, ((3, 4), (5, None)), (((2, 3), ((2, 2),)),))

    def settle(rows, cols):
        for piece in range(2):
            for slot in rows:
                row_copy(slot, piece).wait_recv()
            for slot in cols:
                pair_copy(slot, piece).wait_recv()

    def prepare_rows(chunk):
        for place in range(4):
            norm = jnp.zeros((FRAMES, 1), jnp.float32)
            for comp in range(3):
                value = rbuf[4 * chunk + place, comp * FRAMES:(comp + 1) * FRAMES, :]
                norm = norm + jnp.sum(value * value, axis=1, keepdims=True)
                high, low = split(value)
                at = pl.ds(comp * 128 + place * FRAMES, FRAMES)
                rsplit[chunk, at, 0:256] = high
                rsplit[chunk, at, 256:512] = high
                rsplit[chunk, at, 512:768] = low
            rnorm[chunk, place * FRAMES:(place + 1) * FRAMES, :] = jnp.broadcast_to(0.25 * norm, (FRAMES, 128))

    def prepare_cols(group):
        for place in range(4):
            kind, slot = place // 2, COL_GROUPS[group][place % 2]
            norm = jnp.zeros((FRAMES, 1), jnp.float32)
            for comp in range(3):
                value = cbuf[kind, slot, comp * FRAMES:(comp + 1) * FRAMES, :]
                norm = norm + jnp.sum(value * value, axis=1, keepdims=True)
                high, low = split(value)
                at = pl.ds(comp * 128 + place * FRAMES, FRAMES)
                csplit[group, at, 0:256] = high
                csplit[group, at, 256:512] = low
                csplit[group, at, 512:768] = high
            square_buf[place * FRAMES:(place + 1) * FRAMES, :] = jnp.broadcast_to(norm, (FRAMES, 128))
            for half in range(2):
                value = cbuf[kind, slot, 96:112, half * 128:(half + 1) * 128]
                high, low = split(value)
                start = place * FRAMES + half * 16
                vsplit[group, start:start + 16, :] = high
                vsplit[group, 128 + start:128 + start + 16, :] = high
                vsplit[group, 256 + start:256 + start + 16, :] = low
        cnorm[group] = square_buf[...].T[0:8, :]

    def share(chunk):
        for place in range(4):
            at = 4 * chunk + place
            value = acc[chunk, place * FRAMES:(place + 1) * FRAMES, :]
            if at == 0:
                landed[0] = value
            else:
                parts[at] = value
                share_copy(at).start()

    moments, ksplit = (moments_a, moments_b), (ksplit_a, ksplit_b)
    started, flight = set(), {"moments": None, "values": None, "count": 0}

    def advance(unit):
        count = flight["count"]
        if unit is not None:
            moments[count % 2][...] = lax.dot_general(
                rsplit[unit[0]], csplit[unit[1]], (((1,), (1,)), ((), ())),
                preferred_element_type=jnp.float32,
            )
        valued = flight["values"]
        if valued is not None:
            chunk, group = valued
            added = jnp.dot(ksplit[count % 2][...], vsplit[group], preferred_element_type=jnp.float32)
            acc[chunk] = acc[chunk] + added if chunk in started else added
            started.add(chunk)
        ready = flight["moments"]
        if ready is not None:
            chunk, group = ready
            held, into = moments[(count + 1) % 2], ksplit[(count + 1) % 2]
            col_norm = cnorm[group][0:1, :]
            for start in range(0, 128, SLICE):
                moment = [
                    held[first * 128 + start:first * 128 + start + SLICE, second * 128:(second + 1) * 128]
                    for first in range(3) for second in range(3)
                ]
                values = kernel_values(moment, rnorm[chunk, start:start + SLICE, :], col_norm)
                high, low = split(values)
                into[start:start + SLICE, 0:128] = high
                into[start:start + SLICE, 128:256] = low
                into[start:start + SLICE, 256:384] = high
        if valued is not None and valued[1] == 3:
            share(valued[0])
        flight["moments"], flight["values"], flight["count"] = unit, ready, count + 1

    for piece in range(2):
        first_round(piece)
    settle((), (1, 7))
    prepare_rows(0)
    prepare_cols(0)
    second_round(0)
    advance(UNITS[0][0])
    second_round(1)
    settle(((0, 3), (1, 3)), ())
    prepare_rows(1)
    advance(UNITS[1][0])
    third_round(0)
    settle((), (2, 6))
    prepare_cols(1)
    advance(UNITS[1][1])
    third_round(1)
    advance(UNITS[1][2])
    settle(((3, 1), (0, 2), (2, 1)), ())
    prepare_rows(2)
    for at, unit in enumerate(UNITS[2]):
        if at == 2:
            settle((), (3, 5))
            prepare_cols(2)
        advance(unit)
        if 1 <= at <= 2:
            col_copy(4, at - 1).wait_recv()
            pair_copy(4, at - 1).start()
    settle(((1, 2), (3, 2), (2, 2)), ())
    prepare_rows(3)
    for at, unit in enumerate(UNITS[3]):
        if at == 3:
            settle((), (0, 4))
            prepare_cols(3)
        advance(unit)
    advance(None)
    advance(None)

    for piece in range(2):
        for slot in ROW_SLOTS[1:]:
            row_copy(slot, piece).wait_send()
        for slot in range(1, 8):
            col_copy(slot, piece).wait_send()
        for slot in range(8):
            pair_copy(slot, piece).wait_send()
    total = landed[0]
    for at in range(15, 0, -1):
        share_copy(at).wait_recv()
        total = total + landed[at]
    out_ref[...] = (total / total[:, 64:65])[:, 0:64]
    for at in range(1, 16):
        share_copy(at).wait_send()


def per_device(row_frames, col_frames, vectors):
    vmem = pl.BlockSpec(memory_space=pltpu.VMEM)
    dma = pltpu.SemaphoreType.DMA
    return pl.pallas_call(
        body,
        name="qcp_product",
        out_shape=jax.ShapeDtypeStruct(vectors.shape[::-1], jnp.float32),
        in_specs=[pl.BlockSpec(memory_space=pltpu.HBM)] * 3,
        out_specs=vmem,
        scratch_shapes=[
            pltpu.VMEM(row_frames.shape, jnp.float32),
            pltpu.VMEM(col_frames.shape, jnp.float32),
            pltpu.VMEM(vectors.shape[::-1], jnp.float32),
            pltpu.VMEM((16, 96, ATOMS), jnp.float32),
            pltpu.VMEM((2, 8, 112, ATOMS), jnp.float32),
            pltpu.VMEM((4, 384, 768), jnp.bfloat16),
            pltpu.VMEM((4, 384, 768), jnp.bfloat16),
            pltpu.VMEM((4, 384, 128), jnp.bfloat16),
            pltpu.VMEM((4, 128, 128), jnp.float32),
            pltpu.VMEM((4, 8, 128), jnp.float32),
            pltpu.VMEM((384, 384), jnp.float32),
            pltpu.VMEM((384, 384), jnp.float32),
            pltpu.VMEM((128, 384), jnp.bfloat16),
            pltpu.VMEM((128, 384), jnp.bfloat16),
            pltpu.VMEM((4, 128, 128), jnp.float32),
            pltpu.VMEM((16, FRAMES, 128), jnp.float32),
            pltpu.VMEM((16, FRAMES, 128), jnp.float32),
            pltpu.VMEM((128, 128), jnp.float32),
            dma((3,)), dma((16, 2)), dma((16, 2)), dma((8, 2)), dma((8, 2)),
            dma((8, 2)), dma((8, 2)), dma((16,)), dma((16,)),
        ],
        compiler_params=pltpu.CompilerParams(
            collective_id=0, has_side_effects=True, vmem_limit_bytes=67043328,
        ),
    )(row_frames, col_frames, vectors.T).T


def solution(mesh):
    return jax.shard_map(
        per_device,
        mesh=mesh,
        in_specs=(
            P(None, ("row", "col"), None),
            P(None, ("col", "row"), None),
            P(None, ("col", "row")),
        ),
        out_specs=P(None, ("row", "col")),
        check_vma=False,
    )
```
